256 devices in a mesh: node: 16 (over x, y), tile: 16 (over z, core).
Axes of the slice: x: 4, y: 4, z: 8, core: 2. Of those that a mesh axis runs over, the one named last changes fastest.
Arguments:
- schur: float32 [16, 1536, 24576], P(None, 'tile', 'node'), may hold values from -0.0390625 to 0.0390625
- samples: float32 [16, 1536, 512], P(None, 'tile'), may hold values from -6 to 6
Outputs:
- leaf_basis: float32 [16, 1536, 512], P('node', 'tile')
- level_one: float32 [16, 512, 512], P('node', 'tile')
- level_two: float32 [16, 512, 512], P('node', 'tile')
The draws below stay inside these ranges and needn't reach their ends.
All inputs are finite; a program needn't handle non-finite values.
Results may differ from the reference program's by a relative error of at most 0.00011.
Values sent between devices are 32-bit elements; how exact they have to be, the bound alone decides.
A program may use at most 128 MiB of HBM per device.

```python
import math
import jax
import jax.numpy as jnp
from jax import lax

LEAF = 1536
SAMPLES = 512
LEAVES = 16
ORDER = 24576


def block_levels(stream_key, dims, shards, least, high):
    gain, own = 1.0, jax.random.fold_in(stream_key, 6)
    for dim, blocks in shards:
        heights = jnp.exp(jax.random.uniform(jax.random.fold_in(own, dim), (blocks,), jnp.float32, least / len(shards), high / len(shards)))
        gain = gain * jnp.repeat(heights, dims[dim] // blocks).reshape([-1 if axis == dim else 1 for axis in range(len(dims))])
    return gain


def bell_draw(key, extent, deviation, bound, shards=(), kind=jnp.bfloat16):
    result = jax.random.normal(key, extent, jnp.float32) * deviation
    if len(shards) > 0:
        result = block_levels(key, extent, shards, -0.22, 0.18) * result
    return jnp.clip(result, min=-bound, max=bound).astype(kind)


def setup_inputs(seed: int = 0) -> dict:
    keys = jax.random.split(jax.random.key(seed), 3)
    schur = bell_draw(keys[0], (LEAVES, LEAF, ORDER), ORDER ** -0.5, 0.0390625, ((1, 16), (2, 16)), jnp.float32)
    samples = bell_draw(keys[1], (LEAVES, LEAF, SAMPLES), 1.0, 6.0, ((1, 16),), jnp.float32)
    return dict(schur=schur, samples=samples)


HIGH = lax.Precision.HIGHEST

def product(left, right):
    return jnp.dot(left.astype(jnp.float32), right.astype(jnp.float32), precision=HIGH, preferred_element_type=jnp.float32)

def transposed(left, right):
    return lax.dot_general(left.astype(jnp.float32), right.astype(jnp.float32), (((0,), (0,)), ((), ())), precision=HIGH, preferred_element_type=jnp.float32)

def solve_right(factor, rows):
    return jax.scipy.linalg.solve_triangular(factor, rows.T, lower=True).T

def block_times(schur, row_leaf, col_leaf, panel):
    stored = schur[col_leaf][:, row_leaf * LEAF:(row_leaf + 1) * LEAF]
    return transposed(stored, panel)

def reference(schur, samples):
    matrix = schur.reshape(ORDER, ORDER)
    flat = samples.reshape(ORDER, SAMPLES)
    full = transposed(matrix, flat).reshape(LEAVES, LEAF, SAMPLES)
    basis = []
    factors = []
    reduced = []
    for leaf_index in range(LEAVES):
        local = full[leaf_index] - block_times(schur, leaf_index, leaf_index, samples[leaf_index])
        factor = jnp.linalg.cholesky(transposed(local, local))
        leaf_rows = solve_right(factor, local)
        basis.append(leaf_rows)
        factors.append(factor)
        reduced.append(transposed(leaf_rows, samples[leaf_index]))
    parent_sample = []
    for leaf_index in range(LEAVES):
        sibling = leaf_index ^ 1
        panel = product(basis[sibling], reduced[sibling])
        near = transposed(basis[leaf_index], block_times(schur, leaf_index, sibling, panel))
        parent_sample.append(factors[leaf_index].T - near)
    transfer = [None] * LEAVES
    parent_factor = []
    parent_reduced = []
    for parent in range(LEAVES // 2):
        first, second = (2 * parent, 2 * parent + 1)
        gram = transposed(parent_sample[first], parent_sample[first]) + transposed(parent_sample[second], parent_sample[second])
        factor = jnp.linalg.cholesky(gram)
        parent_factor.append(factor)
        transfer[first] = solve_right(factor, parent_sample[first])
        transfer[second] = solve_right(factor, parent_sample[second])
        parent_reduced.append(transposed(transfer[first], reduced[first]) + transposed(transfer[second], reduced[second]))
    panels = [product(basis[x], product(transfer[x], parent_reduced[x // 2])) for x in range(LEAVES)]
    far = []
    for leaf_index in range(LEAVES):
        cousin_c, cousin_d = (leaf_index ^ 2, leaf_index ^ 3)
        summed = block_times(schur, leaf_index, cousin_c, panels[cousin_c]) + block_times(schur, leaf_index, cousin_d, panels[cousin_d])
        far.append(transposed(transfer[leaf_index], transposed(basis[leaf_index], summed)))
    grand_sample = [parent_factor[p].T - (far[2 * p] + far[2 * p + 1]) for p in range(LEAVES // 2)]
    grand_transfer = [None] * (LEAVES // 2)
    for grand in range(LEAVES // 4):
        first, second = (2 * grand, 2 * grand + 1)
        gram = transposed(grand_sample[first], grand_sample[first]) + transposed(grand_sample[second], grand_sample[second])
        factor = jnp.linalg.cholesky(gram)
        grand_transfer[first] = solve_right(factor, grand_sample[first])
        grand_transfer[second] = solve_right(factor, grand_sample[second])
    leaf_basis = jnp.stack(basis) * math.sqrt(LEAF)
    level_one = jnp.stack(transfer) * math.sqrt(2 * SAMPLES)
    level_two = jnp.stack([product(transfer[x], grand_transfer[x // 2]) for x in range(LEAVES)]) * (2.0 * math.sqrt(SAMPLES))
    return (leaf_basis, level_one, level_two)
```

```python
import math

import jax
import jax.numpy as jnp
from jax import lax
from jax.sharding import PartitionSpec as P

HIGH = lax.Precision.HIGHEST


def swap(block, axis, mask):
    count = lax.axis_size(axis)
    return lax.ppermute(block, axis, [(low, low ^ mask) for low in range(count)])


def product(left, right):
    return jnp.dot(left, right, precision=HIGH, preferred_element_type=jnp.float32)


def transposed(left, right):
    return lax.dot_general(
        left, right, (((0,), (0,)), ((), ())), precision=HIGH, preferred_element_type=jnp.float32
    )


def inverse_lower(factor):
    eye = jnp.eye(factor.shape[0], dtype=factor.dtype)
    return jax.scipy.linalg.solve_triangular(factor, eye, lower=True)


def tile_bits():
    return [bit for bit in range(lax.axis_size("tile").bit_length() - 1)]


def halve(block):
    tile = lax.axis_index("tile")
    for bit in tile_bits():
        side = (tile >> bit) & 1
        half = block.shape[0] // 2
        keep = lax.dynamic_slice_in_dim(block, side * half, half, 0)
        send = lax.dynamic_slice_in_dim(block, (1 - side) * half, half, 0)
        block = keep + swap(send, "tile", 1 << bit)
    return block


def double(block, dim):
    tile = lax.axis_index("tile")
    for bit in reversed(tile_bits()):
        side = (tile >> bit) & 1
        other = swap(block, "tile", 1 << bit)
        block = jnp.where(
            side == 0,
            jnp.concatenate([block, other], axis=dim),
            jnp.concatenate([other, block], axis=dim),
        )
    return block


def chunk_rows(block, count):
    tile = lax.axis_index("tile")
    start = 0
    size = block.shape[0]
    for bit in tile_bits():
        size //= 2
        start = start + ((tile >> bit) & 1) * size
    return lax.dynamic_slice_in_dim(block, start, count, 0)


def on_device(schur, samples):
    leaves, slice_cols, leaf_rows = schur.shape
    rank_size = samples.shape[2]
    node = lax.axis_index("node")
    tile = lax.axis_index("tile")
    tile_count = lax.axis_size("tile")
    out_rows = rank_size // tile_count
    owned = lax.dynamic_index_in_dim(samples, node, 0, keepdims=False)
    keep = (jnp.arange(leaves, dtype=jnp.int32) != node)[:, None, None]
    masked = jnp.where(keep, samples, 0.0).reshape(leaves * slice_cols, rank_size)
    stacked = schur.reshape(leaves * slice_cols, leaf_rows)
    sample_rows = lax.psum_scatter(
        transposed(stacked, masked), "tile", scatter_dimension=0, tiled=True
    )
    both = lax.all_gather(
        jnp.concatenate([sample_rows, owned], axis=1), "tile", axis=0, tiled=True
    )
    local = both[:, :rank_size]
    omega = both[:, rank_size:]
    factor = jnp.linalg.cholesky(transposed(local, local))
    basis = product(local, inverse_lower(factor).T)
    reduced = transposed(basis, omega)
    basis_rows = lax.dynamic_slice_in_dim(basis, tile * slice_cols, slice_cols, 0)

    def meet(target):
        piece = lax.dynamic_index_in_dim(schur, target, 0, keepdims=False)
        return product(piece, basis)

    panel_one = product(basis_rows, reduced)
    sibling_rows = swap(panel_one, "node", 1)
    other_reduced = swap(reduced, "node", 1)
    near_meet = meet(jnp.bitwise_xor(node, 1))
    cousin_meet = meet(jnp.bitwise_xor(node, 2))
    further_meet = meet(jnp.bitwise_xor(node, 3))

    near_part = halve(transposed(near_meet, sibling_rows))
    sample_part = chunk_rows(factor.T, near_part.shape[0]) - near_part
    other_part = swap(sample_part, "node", 1)
    pair = double(jnp.stack([sample_part, other_part]), 1)
    parent_sample, other_sample = pair[0], pair[1]
    parent_factor = jnp.linalg.cholesky(
        transposed(parent_sample, parent_sample) + transposed(other_sample, other_sample)
    )
    parent_inverse = inverse_lower(parent_factor).T
    transfer_own = product(parent_sample, parent_inverse)
    transfer_other = product(other_sample, parent_inverse)
    parent_reduced = transposed(transfer_own, reduced) + transposed(transfer_other, other_reduced)
    panel_two = product(basis_rows, product(transfer_own, parent_reduced))
    cousin_rows = swap(panel_two, "node", 2)
    further_rows = swap(panel_two, "node", 3)
    far_sum = transposed(cousin_meet, cousin_rows) + transposed(further_meet, further_rows)
    far_part = halve(transposed(transfer_own, far_sum))
    far_pair = far_part + swap(far_part, "node", 1)
    grand_part = chunk_rows(parent_factor.T, far_pair.shape[0]) - far_pair
    cousin_part = swap(grand_part, "node", 2)
    grand_pair = double(jnp.stack([grand_part, cousin_part]), 1)
    grand_sample, cousin_grand = grand_pair[0], grand_pair[1]
    grand_factor = jnp.linalg.cholesky(
        transposed(grand_sample, grand_sample) + transposed(cousin_grand, cousin_grand)
    )
    grand_transfer = product(grand_sample, inverse_lower(grand_factor).T)
    leaf_out = (basis_rows * math.sqrt(leaf_rows))[None]
    one_rows = lax.dynamic_slice_in_dim(transfer_own, tile * out_rows, out_rows, 0)
    level_one = (one_rows * math.sqrt(2 * rank_size))[None]
    two_rows = product(one_rows, grand_transfer)
    level_two = (two_rows * (2.0 * math.sqrt(rank_size)))[None]
    return (leaf_out, level_one, level_two)


def solution(mesh):
    placed = (P(None, "tile", "node"), P(None, "tile", None))
    return jax.shard_map(
        on_device,
        mesh=mesh,
        in_specs=placed,
        out_specs=(P("node", "tile", None), P("node", "tile", None), P("node", "tile", None)),
        check_vma=False,
    )
```

```python
import functools
import math

import jax
import jax.numpy as jnp
from jax import lax
from jax.experimental import pallas as pl
from jax.experimental.pallas import tpu as pltpu
from jax.sharding import PartitionSpec as P

HIGH = lax.Precision.HIGHEST


def swap(block, axis, mask):
    count = lax.axis_size(axis)
    return lax.ppermute(block, axis, [(low, low ^ mask) for low in range(count)])


def product(left, right):
    return jnp.dot(left, right, precision=HIGH, preferred_element_type=jnp.float32)


def transposed(left, right):
    return lax.dot_general(
        left, right, (((0,), (0,)), ((), ())), precision=HIGH, preferred_element_type=jnp.float32
    )


def inverse_lower(factor):
    eye = jnp.eye(factor.shape[0], dtype=factor.dtype)
    return jax.scipy.linalg.solve_triangular(factor, eye, lower=True)


MESH = pl.DeviceIdType.MESH
VMEM = pltpu.VMEM


def greet(count):
    me = lax.axis_index("tile")
    barrier = pltpu.get_barrier_semaphore()
    for step in range(1, count):
        pl.semaphore_signal(
            barrier, inc=1, device_id={"tile": lax.rem(me + step, count)}, device_id_type=MESH
        )
    pl.semaphore_wait(barrier, count - 1)
    return me


def scatter_kernel(count, block_ref, out_ref, held, send_sem, recv_sem):
    me = greet(count)
    rows = out_ref.shape[0]
    copies = []
    for step in range(1, count):
        target = lax.rem(me + step, count)
        copy = pltpu.make_async_remote_copy(
            src_ref=block_ref.at[pl.ds(pl.multiple_of(target * rows, 8), rows)],
            dst_ref=held.at[step],
            send_sem=send_sem.at[step],
            recv_sem=recv_sem.at[step],
            device_id={"tile": target},
            device_id_type=MESH,
        )
        copy.start()
        copies.append(copy)
    total = block_ref[pl.ds(pl.multiple_of(me * rows, 8), rows), :]
    for step, copy in zip(range(1, count), copies):
        copy.wait()
        total = total + held[step]
    out_ref[...] = total


def gather_kernel(count, block_ref, out_ref, held, send_sem, recv_sem):
    me = greet(count)
    rows = block_ref.shape[0]
    copies = []
    for step in range(1, count):
        target = lax.rem(me + step, count)
        copy = pltpu.make_async_remote_copy(
            src_ref=block_ref,
            dst_ref=held.at[pl.ds(pl.multiple_of(me * rows, 8), rows)],
            send_sem=send_sem.at[step],
            recv_sem=recv_sem.at[step],
            device_id={"tile": target},
            device_id_type=MESH,
        )
        copy.start()
        copies.append(copy)
    out_ref[pl.ds(pl.multiple_of(me * rows, 8), rows), :] = block_ref[...]
    for step, copy in zip(range(1, count), copies):
        copy.wait()
        source = lax.rem(me + count - step, count)
        out_ref[pl.ds(pl.multiple_of(source * rows, 8), rows), :] = held[
            pl.ds(pl.multiple_of(source * rows, 8), rows), :
        ]


def tile_scatter(block, ident):
    count = lax.axis_size("tile")
    rows = block.shape[0] // count
    return pl.pallas_call(
        functools.partial(scatter_kernel, count),
        out_shape=jax.ShapeDtypeStruct((rows, block.shape[1]), block.dtype),
        in_specs=[pl.BlockSpec(memory_space=VMEM)],
        out_specs=pl.BlockSpec(memory_space=VMEM),
        scratch_shapes=[
            VMEM((count, rows, block.shape[1]), block.dtype),
            pltpu.SemaphoreType.DMA((count,)),
            pltpu.SemaphoreType.DMA((count,)),
        ],
        compiler_params=pltpu.CompilerParams(
            collective_id=ident, has_side_effects=True
        ),
    )(block)


def tile_gather(block, ident):
    count = lax.axis_size("tile")
    shape = (block.shape[0] * count, block.shape[1])
    return pl.pallas_call(
        functools.partial(gather_kernel, count),
        out_shape=jax.ShapeDtypeStruct(shape, block.dtype),
        in_specs=[pl.BlockSpec(memory_space=VMEM)],
        out_specs=pl.BlockSpec(memory_space=VMEM),
        scratch_shapes=[
            VMEM(shape, block.dtype),
            pltpu.SemaphoreType.DMA((count,)),
            pltpu.SemaphoreType.DMA((count,)),
        ],
        compiler_params=pltpu.CompilerParams(
            collective_id=ident, has_side_effects=True
        ),
    )(block)


def on_device(schur, samples):
    leaves, slice_cols, leaf_rows = schur.shape
    rank_size = samples.shape[2]
    node = lax.axis_index("node")
    tile = lax.axis_index("tile")
    tile_count = lax.axis_size("tile")
    out_rows = rank_size // tile_count
    owned = lax.dynamic_index_in_dim(samples, node, 0, keepdims=False)
    keep = (jnp.arange(leaves, dtype=jnp.int32) != node)[:, None, None]
    masked = jnp.where(keep, samples, 0.0).reshape(leaves * slice_cols, rank_size)
    stacked = schur.reshape(leaves * slice_cols, leaf_rows)
    sample_rows = tile_scatter(transposed(stacked, masked), 1)
    both = tile_gather(jnp.concatenate([sample_rows, owned], axis=1), 2)
    local = both[:, :rank_size]
    omega = both[:, rank_size:]
    factor = jnp.linalg.cholesky(transposed(local, local))
    basis = product(local, inverse_lower(factor).T)
    reduced = transposed(basis, omega)
    basis_rows = lax.dynamic_slice_in_dim(basis, tile * slice_cols, slice_cols, 0)

    def meet(target):
        piece = lax.dynamic_index_in_dim(schur, target, 0, keepdims=False)
        return product(piece, basis)

    panel_one = product(basis_rows, reduced)
    sibling_rows = swap(panel_one, "node", 1)
    other_reduced = swap(reduced, "node", 1)
    near_meet = meet(jnp.bitwise_xor(node, 1))
    cousin_meet = meet(jnp.bitwise_xor(node, 2))
    further_meet = meet(jnp.bitwise_xor(node, 3))

    near_part = tile_scatter(transposed(near_meet, sibling_rows), 3)
    chunk = near_part.shape[0]
    sample_part = lax.dynamic_slice_in_dim(factor.T, tile * chunk, chunk, 0) - near_part
    other_part = swap(sample_part, "node", 1)
    pair = tile_gather(jnp.concatenate([sample_part, other_part], axis=1), 4)
    parent_sample, other_sample = pair[:, :rank_size], pair[:, rank_size:]
    parent_factor = jnp.linalg.cholesky(
        transposed(parent_sample, parent_sample) + transposed(other_sample, other_sample)
    )
    parent_inverse = inverse_lower(parent_factor).T
    transfer_own = product(parent_sample, parent_inverse)
    transfer_other = product(other_sample, parent_inverse)
    parent_reduced = transposed(transfer_own, reduced) + transposed(transfer_other, other_reduced)
    panel_two = product(basis_rows, product(transfer_own, parent_reduced))
    cousin_rows = swap(panel_two, "node", 2)
    further_rows = swap(panel_two, "node", 3)
    far_sum = transposed(cousin_meet, cousin_rows) + transposed(further_meet, further_rows)
    far_part = tile_scatter(transposed(transfer_own, far_sum), 5)
    far_pair = far_part + swap(far_part, "node", 1)
    grand_part = lax.dynamic_slice_in_dim(parent_factor.T, tile * chunk, chunk, 0) - far_pair
    cousin_part = swap(grand_part, "node", 2)
    grand_pair = tile_gather(jnp.concatenate([grand_part, cousin_part], axis=1), 6)
    grand_sample, cousin_grand = grand_pair[:, :rank_size], grand_pair[:, rank_size:]
    grand_factor = jnp.linalg.cholesky(
        transposed(grand_sample, grand_sample) + transposed(cousin_grand, cousin_grand)
    )
    grand_transfer = product(grand_sample, inverse_lower(grand_factor).T)
    leaf_out = (basis_rows * math.sqrt(leaf_rows))[None]
    one_rows = lax.dynamic_slice_in_dim(transfer_own, tile * out_rows, out_rows, 0)
    level_one = (one_rows * math.sqrt(2 * rank_size))[None]
    two_rows = product(one_rows, grand_transfer)
    level_two = (two_rows * (2.0 * math.sqrt(rank_size)))[None]
    return (leaf_out, level_one, level_two)


def solution(mesh):
    placed = (P(None, "tile", "node"), P(None, "tile", None))
    return jax.shard_map(
        on_device,
        mesh=mesh,
        in_specs=placed,
        out_specs=(P("node", "tile", None), P("node", "tile", None), P("node", "tile", None)),
        check_vma=False,
    )
```

```python
import functools
import math

import jax
import jax.numpy as jnp
from jax import lax
from jax.experimental import pallas as pl
from jax.experimental.pallas import tpu as pltpu
from jax.sharding import PartitionSpec as P

HIGH = lax.Precision.HIGHEST


def swap(block, axis, mask):
    count = lax.axis_size(axis)
    return lax.ppermute(block, axis, [(low, low ^ mask) for low in range(count)])


def product(left, right):
    return jnp.dot(left, right, precision=HIGH, preferred_element_type=jnp.float32)


def transposed(left, right):
    return lax.dot_general(
        left, right, (((0,), (0,)), ((), ())), precision=HIGH, preferred_element_type=jnp.float32
    )


def inverse_lower(factor):
    eye = jnp.eye(factor.shape[0], dtype=factor.dtype)
    return jax.scipy.linalg.solve_triangular(factor, eye, lower=True)


MESH = pl.DeviceIdType.MESH
VMEM = pltpu.VMEM


def greet(count):
    me = lax.axis_index("tile")
    barrier = pltpu.get_barrier_semaphore()
    for step in range(1, count):
        pl.semaphore_signal(
            barrier, inc=1, device_id={"tile": lax.rem(me + step, count)}, device_id_type=MESH
        )
    pl.semaphore_wait(barrier, count - 1)
    return me


def scatter_kernel(count, block_ref, out_ref, held, send_sem, recv_sem):
    me = greet(count)
    rows = out_ref.shape[0]
    copies = []
    for step in range(1, count):
        target = lax.rem(me + step, count)
        copy = pltpu.make_async_remote_copy(
            src_ref=block_ref.at[pl.ds(pl.multiple_of(target * rows, 8), rows)],
            dst_ref=held.at[step],
            send_sem=send_sem.at[step],
            recv_sem=recv_sem.at[step],
            device_id={"tile": target},
            device_id_type=MESH,
        )
        copy.start()
        copies.append(copy)
    total = block_ref[pl.ds(pl.multiple_of(me * rows, 8), rows), :]
    for step, copy in zip(range(1, count), copies):
        copy.wait()
        total = total + held[step]
    out_ref[...] = total


def gather_kernel(count, block_ref, out_ref, held, send_sem, recv_sem):
    me = greet(count)
    rows = block_ref.shape[0]
    copies = []
    for step in range(1, count):
        target = lax.rem(me + step, count)
        copy = pltpu.make_async_remote_copy(
            src_ref=block_ref,
            dst_ref=held.at[pl.ds(pl.multiple_of(me * rows, 8), rows)],
            send_sem=send_sem.at[step],
            recv_sem=recv_sem.at[step],
            device_id={"tile": target},
            device_id_type=MESH,
        )
        copy.start()
        copies.append(copy)
    out_ref[pl.ds(pl.multiple_of(me * rows, 8), rows), :] = block_ref[...]
    for step, copy in zip(range(1, count), copies):
        copy.wait()
        source = lax.rem(me + count - step, count)
        out_ref[pl.ds(pl.multiple_of(source * rows, 8), rows), :] = held[
            pl.ds(pl.multiple_of(source * rows, 8), rows), :
        ]


def tile_scatter(block, ident):
    count = lax.axis_size("tile")
    rows = block.shape[0] // count
    return pl.pallas_call(
        functools.partial(scatter_kernel, count),
        out_shape=jax.ShapeDtypeStruct((rows, block.shape[1]), block.dtype),
        in_specs=[pl.BlockSpec(memory_space=VMEM)],
        out_specs=pl.BlockSpec(memory_space=VMEM),
        scratch_shapes=[
            VMEM((count, rows, block.shape[1]), block.dtype),
            pltpu.SemaphoreType.DMA((count,)),
            pltpu.SemaphoreType.DMA((count,)),
        ],
        compiler_params=pltpu.CompilerParams(
            collective_id=ident, has_side_effects=True
        ),
    )(block)


def tile_gather(block, ident):
    count = lax.axis_size("tile")
    shape = (block.shape[0] * count, block.shape[1])
    return pl.pallas_call(
        functools.partial(gather_kernel, count),
        out_shape=jax.ShapeDtypeStruct(shape, block.dtype),
        in_specs=[pl.BlockSpec(memory_space=VMEM)],
        out_specs=pl.BlockSpec(memory_space=VMEM),
        scratch_shapes=[
            VMEM(shape, block.dtype),
            pltpu.SemaphoreType.DMA((count,)),
            pltpu.SemaphoreType.DMA((count,)),
        ],
        compiler_params=pltpu.CompilerParams(
            collective_id=ident, has_side_effects=True
        ),
    )(block)


def on_device(schur, samples):
    leaves, slice_cols, leaf_rows = schur.shape
    rank_size = samples.shape[2]
    node = lax.axis_index("node")
    tile = lax.axis_index("tile")
    tile_count = lax.axis_size("tile")
    out_rows = rank_size // tile_count
    owned = lax.dynamic_index_in_dim(samples, node, 0, keepdims=False)
    keep = (jnp.arange(leaves, dtype=jnp.int32) != node)[:, None, None]
    masked = jnp.where(keep, samples, 0.0).reshape(leaves * slice_cols, rank_size)
    stacked = schur.reshape(leaves * slice_cols, leaf_rows)
    sample_rows = lax.psum_scatter(
        transposed(stacked, masked), "tile", scatter_dimension=0, tiled=True
    )
    both = lax.all_gather(
        jnp.concatenate([sample_rows, owned], axis=1), "tile", axis=0, tiled=True
    )
    local = both[:, :rank_size]
    omega = both[:, rank_size:]
    factor = jnp.linalg.cholesky(transposed(local, local))
    basis = product(local, inverse_lower(factor).T)
    reduced = transposed(basis, omega)
    basis_rows = lax.dynamic_slice_in_dim(basis, tile * slice_cols, slice_cols, 0)

    def meet(target):
        piece = lax.dynamic_index_in_dim(schur, target, 0, keepdims=False)
        return product(piece, basis)

    panel_one = product(basis_rows, reduced)
    sibling_rows = swap(panel_one, "node", 1)
    other_reduced = swap(reduced, "node", 1)
    near_meet = meet(jnp.bitwise_xor(node, 1))
    cousin_meet = meet(jnp.bitwise_xor(node, 2))
    further_meet = meet(jnp.bitwise_xor(node, 3))

    near_part = tile_scatter(transposed(near_meet, sibling_rows), 3)
    chunk = near_part.shape[0]
    sample_part = lax.dynamic_slice_in_dim(factor.T, tile * chunk, chunk, 0) - near_part
    other_part = swap(sample_part, "node", 1)
    pair = tile_gather(jnp.concatenate([sample_part, other_part], axis=1), 4)
    parent_sample, other_sample = pair[:, :rank_size], pair[:, rank_size:]
    parent_factor = jnp.linalg.cholesky(
        transposed(parent_sample, parent_sample) + transposed(other_sample, other_sample)
    )
    parent_inverse = inverse_lower(parent_factor).T
    transfer_own = product(parent_sample, parent_inverse)
    transfer_other = product(other_sample, parent_inverse)
    parent_reduced = transposed(transfer_own, reduced) + transposed(transfer_other, other_reduced)
    panel_two = product(basis_rows, product(transfer_own, parent_reduced))
    cousin_rows = swap(panel_two, "node", 2)
    further_rows = swap(panel_two, "node", 3)
    far_sum = transposed(cousin_meet, cousin_rows) + transposed(further_meet, further_rows)
    far_part = tile_scatter(transposed(transfer_own, far_sum), 5)
    far_pair = far_part + swap(far_part, "node", 1)
    grand_part = lax.dynamic_slice_in_dim(parent_factor.T, tile * chunk, chunk, 0) - far_pair
    cousin_part = swap(grand_part, "node", 2)
    grand_pair = tile_gather(jnp.concatenate([grand_part, cousin_part], axis=1), 6)
    grand_sample, cousin_grand = grand_pair[:, :rank_size], grand_pair[:, rank_size:]
    grand_factor = jnp.linalg.cholesky(
        transposed(grand_sample, grand_sample) + transposed(cousin_grand, cousin_grand)
    )
    grand_transfer = product(grand_sample, inverse_lower(grand_factor).T)
    leaf_out = (basis_rows * math.sqrt(leaf_rows))[None]
    one_rows = lax.dynamic_slice_in_dim(transfer_own, tile * out_rows, out_rows, 0)
    level_one = (one_rows * math.sqrt(2 * rank_size))[None]
    two_rows = product(one_rows, grand_transfer)
    level_two = (two_rows * (2.0 * math.sqrt(rank_size)))[None]
    return (leaf_out, level_one, level_two)


def solution(mesh):
    placed = (P(None, "tile", "node"), P(None, "tile", None))
    return jax.shard_map(
        on_device,
        mesh=mesh,
        in_specs=placed,
        out_specs=(P("node", "tile", None), P("node", "tile", None), P("node", "tile", None)),
        check_vma=False,
    )
```

```python
import functools
import math

import jax
import jax.numpy as jnp
from jax import lax
from jax.experimental import pallas as pl
from jax.experimental.pallas import tpu as pltpu
from jax.sharding import PartitionSpec as P

HIGH = lax.Precision.HIGHEST


def swap(block, axis, mask):
    count = lax.axis_size(axis)
    return lax.ppermute(block, axis, [(low, low ^ mask) for low in range(count)])


def product(left, right):
    return jnp.dot(left, right, precision=HIGH, preferred_element_type=jnp.float32)


def transposed(left, right):
    return lax.dot_general(
        left, right, (((0,), (0,)), ((), ())), precision=HIGH, preferred_element_type=jnp.float32
    )


def inverse_lower(factor):
    eye = jnp.eye(factor.shape[0], dtype=factor.dtype)
    return jax.scipy.linalg.solve_triangular(factor, eye, lower=True)


def join_lower(upper_left, lower_left, lower_right):
    top = jnp.concatenate([upper_left, jnp.zeros_like(upper_left)], axis=1)
    return jnp.concatenate([top, jnp.concatenate([lower_left, lower_right], axis=1)], axis=0)


def factor_pair(gram, block=128):
    size = gram.shape[0]
    panels = []
    inverses = []
    for start in range(0, size, block):
        stop = start + block
        column = gram[start:, start:stop]
        if panels:
            done = jnp.concatenate(panels, axis=1)
            column = column - product(done[start:], done[start:stop].T)
        diagonal = jnp.linalg.cholesky(column[:block])
        inverse = inverse_lower(diagonal)
        inverses.append(inverse)
        below = product(column[block:], inverse.T)
        panel = jnp.concatenate([diagonal, below], axis=0)
        if start:
            panel = jnp.concatenate([jnp.zeros((start, block), gram.dtype), panel], axis=0)
        panels.append(panel)
    factor = jnp.concatenate(panels, axis=1)
    width = block
    while len(inverses) > 1:
        merged = []
        for pair in range(0, len(inverses), 2):
            first, second = inverses[pair], inverses[pair + 1]
            lo = pair * width
            coupling = factor[lo + width:lo + 2 * width, lo:lo + width]
            lower_left = -product(second, product(coupling, first))
            merged.append(join_lower(first, lower_left, second))
        inverses = merged
        width *= 2
    return factor, inverses[0]


MESH = pl.DeviceIdType.MESH
VMEM = pltpu.VMEM


def greet(count):
    me = lax.axis_index("tile")
    barrier = pltpu.get_barrier_semaphore()
    for step in range(1, count):
        pl.semaphore_signal(
            barrier, inc=1, device_id={"tile": lax.rem(me + step, count)}, device_id_type=MESH
        )
    pl.semaphore_wait(barrier, count - 1)
    return me


def scatter_kernel(count, block_ref, out_ref, held, send_sem, recv_sem):
    me = greet(count)
    rows = out_ref.shape[0]
    copies = []
    for step in range(1, count):
        target = lax.rem(me + step, count)
        copy = pltpu.make_async_remote_copy(
            src_ref=block_ref.at[pl.ds(pl.multiple_of(target * rows, 8), rows)],
            dst_ref=held.at[step],
            send_sem=send_sem.at[step],
            recv_sem=recv_sem.at[step],
            device_id={"tile": target},
            device_id_type=MESH,
        )
        copy.start()
        copies.append(copy)
    total = block_ref[pl.ds(pl.multiple_of(me * rows, 8), rows), :]
    for step, copy in zip(range(1, count), copies):
        copy.wait()
        total = total + held[step]
    out_ref[...] = total


def gather_kernel(count, block_ref, out_ref, held, send_sem, recv_sem):
    me = greet(count)
    rows = block_ref.shape[0]
    copies = []
    for step in range(1, count):
        target = lax.rem(me + step, count)
        copy = pltpu.make_async_remote_copy(
            src_ref=block_ref,
            dst_ref=held.at[pl.ds(pl.multiple_of(me * rows, 8), rows)],
            send_sem=send_sem.at[step],
            recv_sem=recv_sem.at[step],
            device_id={"tile": target},
            device_id_type=MESH,
        )
        copy.start()
        copies.append(copy)
    out_ref[pl.ds(pl.multiple_of(me * rows, 8), rows), :] = block_ref[...]
    for step, copy in zip(range(1, count), copies):
        copy.wait()
        source = lax.rem(me + count - step, count)
        out_ref[pl.ds(pl.multiple_of(source * rows, 8), rows), :] = held[
            pl.ds(pl.multiple_of(source * rows, 8), rows), :
        ]


def tile_scatter(block, ident):
    count = lax.axis_size("tile")
    rows = block.shape[0] // count
    return pl.pallas_call(
        functools.partial(scatter_kernel, count),
        out_shape=jax.ShapeDtypeStruct((rows, block.shape[1]), block.dtype),
        in_specs=[pl.BlockSpec(memory_space=VMEM)],
        out_specs=pl.BlockSpec(memory_space=VMEM),
        scratch_shapes=[
            VMEM((count, rows, block.shape[1]), block.dtype),
            pltpu.SemaphoreType.DMA((count,)),
            pltpu.SemaphoreType.DMA((count,)),
        ],
        compiler_params=pltpu.CompilerParams(
            collective_id=ident
        ),
    )(block)


def tile_gather(block, ident):
    count = lax.axis_size("tile")
    shape = (block.shape[0] * count, block.shape[1])
    return pl.pallas_call(
        functools.partial(gather_kernel, count),
        out_shape=jax.ShapeDtypeStruct(shape, block.dtype),
        in_specs=[pl.BlockSpec(memory_space=VMEM)],
        out_specs=pl.BlockSpec(memory_space=VMEM),
        scratch_shapes=[
            VMEM(shape, block.dtype),
            pltpu.SemaphoreType.DMA((count,)),
            pltpu.SemaphoreType.DMA((count,)),
        ],
        compiler_params=pltpu.CompilerParams(
            collective_id=ident
        ),
    )(block)


def on_device(schur, samples):
    leaves, slice_cols, leaf_rows = schur.shape
    rank_size = samples.shape[2]
    node = lax.axis_index("node")
    tile = lax.axis_index("tile")
    tile_count = lax.axis_size("tile")
    out_rows = rank_size // tile_count
    owned = lax.dynamic_index_in_dim(samples, node, 0, keepdims=False)
    keep = (jnp.arange(leaves, dtype=jnp.int32) != node)[:, None, None]
    masked = jnp.where(keep, samples, 0.0).reshape(leaves * slice_cols, rank_size)
    stacked = schur.reshape(leaves * slice_cols, leaf_rows)
    sample_rows = lax.psum_scatter(
        transposed(stacked, masked), "tile", scatter_dimension=0, tiled=True
    )
    both = lax.all_gather(
        jnp.concatenate([sample_rows, owned], axis=1), "tile", axis=0, tiled=True
    )
    local = both[:, :rank_size]
    omega = both[:, rank_size:]
    factor, factor_inverse = factor_pair(transposed(local, local))
    basis = product(local, factor_inverse.T)
    reduced = transposed(basis, omega)
    basis_rows = lax.dynamic_slice_in_dim(basis, tile * slice_cols, slice_cols, 0)

    def meet(target):
        piece = lax.dynamic_index_in_dim(schur, target, 0, keepdims=False)
        return product(piece, basis)

    panel_one = product(basis_rows, reduced)
    sibling_rows = swap(panel_one, "node", 1)
    other_reduced = swap(reduced, "node", 1)
    near_meet = meet(jnp.bitwise_xor(node, 1))
    cousin_meet = meet(jnp.bitwise_xor(node, 2))
    further_meet = meet(jnp.bitwise_xor(node, 3))

    near_part = tile_scatter(transposed(near_meet, sibling_rows), 3)
    chunk = near_part.shape[0]
    sample_part = lax.dynamic_slice_in_dim(factor.T, tile * chunk, chunk, 0) - near_part
    other_part = swap(sample_part, "node", 1)
    pair = tile_gather(jnp.concatenate([sample_part, other_part], axis=1), 4)
    parent_sample, other_sample = pair[:, :rank_size], pair[:, rank_size:]
    parent_factor, parent_inverse = factor_pair(
        transposed(parent_sample, parent_sample) + transposed(other_sample, other_sample)
    )
    parent_inverse = parent_inverse.T
    transfer_own = product(parent_sample, parent_inverse)
    transfer_other = product(other_sample, parent_inverse)
    parent_reduced = transposed(transfer_own, reduced) + transposed(transfer_other, other_reduced)
    panel_two = product(basis_rows, product(transfer_own, parent_reduced))
    cousin_rows = swap(panel_two, "node", 2)
    further_rows = swap(panel_two, "node", 3)
    far_sum = transposed(cousin_meet, cousin_rows) + transposed(further_meet, further_rows)
    far_part = tile_scatter(transposed(transfer_own, far_sum), 5)
    far_pair = far_part + swap(far_part, "node", 1)
    grand_part = lax.dynamic_slice_in_dim(parent_factor.T, tile * chunk, chunk, 0) - far_pair
    cousin_part = swap(grand_part, "node", 2)
    grand_pair = tile_gather(jnp.concatenate([grand_part, cousin_part], axis=1), 6)
    grand_sample, cousin_grand = grand_pair[:, :rank_size], grand_pair[:, rank_size:]
    grand_factor, grand_inverse = factor_pair(
        transposed(grand_sample, grand_sample) + transposed(cousin_grand, cousin_grand)
    )
    grand_transfer = product(grand_sample, grand_inverse.T)
    leaf_out = (basis_rows * math.sqrt(leaf_rows))[None]
    one_rows = lax.dynamic_slice_in_dim(transfer_own, tile * out_rows, out_rows, 0)
    level_one = (one_rows * math.sqrt(2 * rank_size))[None]
    two_rows = product(one_rows, grand_transfer)
    level_two = (two_rows * (2.0 * math.sqrt(rank_size)))[None]
    return (leaf_out, level_one, level_two)


def solution(mesh):
    placed = (P(None, "tile", "node"), P(None, "tile", None))
    return jax.shard_map(
        on_device,
        mesh=mesh,
        in_specs=placed,
        out_specs=(P("node", "tile", None), P("node", "tile", None), P("node", "tile", None)),
        check_vma=False,
    )
```

```python
import functools
import math

import jax
import jax.numpy as jnp
from jax import lax
from jax.experimental import pallas as pl
from jax.experimental.pallas import tpu as pltpu
from jax.sharding import PartitionSpec as P

HIGH = lax.Precision.HIGHEST


def swap(block, axis, mask):
    count = lax.axis_size(axis)
    return lax.ppermute(block, axis, [(low, low ^ mask) for low in range(count)])


def product(left, right):
    return jnp.dot(left, right, precision=HIGH, preferred_element_type=jnp.float32)


def transposed(left, right):
    return lax.dot_general(
        left, right, (((0,), (0,)), ((), ())), precision=HIGH, preferred_element_type=jnp.float32
    )


def inverse_lower(factor):
    eye = jnp.eye(factor.shape[0], dtype=factor.dtype)
    return jax.scipy.linalg.solve_triangular(factor, eye, lower=True)


def join_lower(upper_left, lower_left, lower_right):
    top = jnp.concatenate([upper_left, jnp.zeros_like(upper_left)], axis=1)
    return jnp.concatenate([top, jnp.concatenate([lower_left, lower_right], axis=1)], axis=0)


def factor_pair(gram, block=128):
    size = gram.shape[0]
    panels = []
    inverses = []
    for start in range(0, size, block):
        stop = start + block
        column = gram[start:, start:stop]
        if panels:
            done = jnp.concatenate(panels, axis=1)
            column = column - product(done[start:], done[start:stop].T)
        diagonal = jnp.linalg.cholesky(column[:block])
        inverse = inverse_lower(diagonal)
        inverses.append(inverse)
        below = product(column[block:], inverse.T)
        panel = jnp.concatenate([diagonal, below], axis=0)
        if start:
            panel = jnp.concatenate([jnp.zeros((start, block), gram.dtype), panel], axis=0)
        panels.append(panel)
    factor = jnp.concatenate(panels, axis=1)
    width = block
    while len(inverses) > 1:
        merged = []
        for pair in range(0, len(inverses), 2):
            first, second = inverses[pair], inverses[pair + 1]
            lo = pair * width
            coupling = factor[lo + width:lo + 2 * width, lo:lo + width]
            lower_left = -product(second, product(coupling, first))
            merged.append(join_lower(first, lower_left, second))
        inverses = merged
        width *= 2
    return factor, inverses[0]


MESH = pl.DeviceIdType.MESH
VMEM = pltpu.VMEM


def greet(count):
    me = lax.axis_index("tile")
    barrier = pltpu.get_barrier_semaphore()
    for step in range(1, count):
        pl.semaphore_signal(
            barrier, inc=1, device_id={"tile": lax.rem(me + step, count)}, device_id_type=MESH
        )
    pl.semaphore_wait(barrier, count - 1)
    return me


def scatter_kernel(count, block_ref, out_ref, held, send_sem, recv_sem):
    me = greet(count)
    rows = out_ref.shape[0]
    copies = []
    for step in range(1, count):
        target = lax.rem(me + step, count)
        copy = pltpu.make_async_remote_copy(
            src_ref=block_ref.at[pl.ds(pl.multiple_of(target * rows, 8), rows)],
            dst_ref=held.at[step],
            send_sem=send_sem.at[step],
            recv_sem=recv_sem.at[step],
            device_id={"tile": target},
            device_id_type=MESH,
        )
        copy.start()
        copies.append(copy)
    total = block_ref[pl.ds(pl.multiple_of(me * rows, 8), rows), :]
    for step, copy in zip(range(1, count), copies):
        copy.wait()
        total = total + held[step]
    out_ref[...] = total


def gather_kernel(count, block_ref, out_ref, held, send_sem, recv_sem):
    me = greet(count)
    rows = block_ref.shape[0]
    copies = []
    for step in range(1, count):
        target = lax.rem(me + step, count)
        copy = pltpu.make_async_remote_copy(
            src_ref=block_ref,
            dst_ref=held.at[pl.ds(pl.multiple_of(me * rows, 8), rows)],
            send_sem=send_sem.at[step],
            recv_sem=recv_sem.at[step],
            device_id={"tile": target},
            device_id_type=MESH,
        )
        copy.start()
        copies.append(copy)
    out_ref[pl.ds(pl.multiple_of(me * rows, 8), rows), :] = block_ref[...]
    for step, copy in zip(range(1, count), copies):
        copy.wait()
        source = lax.rem(me + count - step, count)
        out_ref[pl.ds(pl.multiple_of(source * rows, 8), rows), :] = held[
            pl.ds(pl.multiple_of(source * rows, 8), rows), :
        ]


def tile_scatter(block, ident):
    count = lax.axis_size("tile")
    rows = block.shape[0] // count
    return pl.pallas_call(
        functools.partial(scatter_kernel, count),
        out_shape=jax.ShapeDtypeStruct((rows, block.shape[1]), block.dtype),
        in_specs=[pl.BlockSpec(memory_space=VMEM)],
        out_specs=pl.BlockSpec(memory_space=VMEM),
        scratch_shapes=[
            VMEM((count, rows, block.shape[1]), block.dtype),
            pltpu.SemaphoreType.DMA((count,)),
            pltpu.SemaphoreType.DMA((count,)),
        ],
        compiler_params=pltpu.CompilerParams(
            collective_id=ident
        ),
    )(block)


def tile_gather(block, ident):
    count = lax.axis_size("tile")
    shape = (block.shape[0] * count, block.shape[1])
    return pl.pallas_call(
        functools.partial(gather_kernel, count),
        out_shape=jax.ShapeDtypeStruct(shape, block.dtype),
        in_specs=[pl.BlockSpec(memory_space=VMEM)],
        out_specs=pl.BlockSpec(memory_space=VMEM),
        scratch_shapes=[
            VMEM(shape, block.dtype),
            pltpu.SemaphoreType.DMA((count,)),
            pltpu.SemaphoreType.DMA((count,)),
        ],
        compiler_params=pltpu.CompilerParams(
            collective_id=ident
        ),
    )(block)


def on_device(schur, samples):
    leaves, slice_cols, leaf_rows = schur.shape
    rank_size = samples.shape[2]
    node = lax.axis_index("node")
    tile = lax.axis_index("tile")
    tile_count = lax.axis_size("tile")
    out_rows = rank_size // tile_count
    owned = lax.dynamic_index_in_dim(samples, node, 0, keepdims=False)
    keep = (jnp.arange(leaves, dtype=jnp.int32) != node)[:, None, None]
    masked = jnp.where(keep, samples, 0.0).reshape(leaves * slice_cols, rank_size)
    stacked = schur.reshape(leaves * slice_cols, leaf_rows)
    sample_rows = lax.psum_scatter(
        transposed(stacked, masked), "tile", scatter_dimension=0, tiled=True
    )
    both = lax.all_gather(
        jnp.concatenate([sample_rows, owned], axis=1), "tile", axis=0, tiled=True
    )
    local = both[:, :rank_size]
    omega = both[:, rank_size:]
    factor, factor_inverse = factor_pair(transposed(local, local))
    basis = product(local, factor_inverse.T)
    reduced = transposed(basis, omega)
    basis_rows = lax.dynamic_slice_in_dim(basis, tile * slice_cols, slice_cols, 0)

    def meet(target):
        piece = lax.dynamic_index_in_dim(schur, target, 0, keepdims=False)
        return product(piece, basis)

    panel_one = product(basis_rows, reduced)
    sibling_rows = swap(panel_one, "node", 1)
    near_meet = meet(jnp.bitwise_xor(node, 1))
    cousin_meet = meet(jnp.bitwise_xor(node, 2))
    further_meet = meet(jnp.bitwise_xor(node, 3))

    near_part = tile_scatter(transposed(near_meet, sibling_rows), 3)
    late_reduced, near_part = lax.optimization_barrier((reduced, near_part))
    other_reduced = swap(late_reduced, "node", 1)
    chunk = near_part.shape[0]
    sample_part = lax.dynamic_slice_in_dim(factor.T, tile * chunk, chunk, 0) - near_part
    other_part = swap(sample_part, "node", 1)
    pair = lax.all_gather(
        jnp.concatenate([sample_part, other_part], axis=1), "tile", axis=0, tiled=True
    )
    parent_sample, other_sample = pair[:, :rank_size], pair[:, rank_size:]
    parent_factor, parent_inverse = factor_pair(
        transposed(parent_sample, parent_sample) + transposed(other_sample, other_sample)
    )
    parent_inverse = parent_inverse.T
    transfer_own = product(parent_sample, parent_inverse)
    transfer_other = product(other_sample, parent_inverse)
    parent_reduced = transposed(transfer_own, reduced) + transposed(transfer_other, other_reduced)
    panel_two = product(basis_rows, product(transfer_own, parent_reduced))
    cousin_rows = swap(panel_two, "node", 2)
    further_rows = swap(panel_two, "node", 3)
    far_sum = transposed(cousin_meet, cousin_rows) + transposed(further_meet, further_rows)
    far_part = tile_scatter(transposed(transfer_own, far_sum), 5)
    far_pair = far_part + swap(far_part, "node", 1)
    grand_part = lax.dynamic_slice_in_dim(parent_factor.T, tile * chunk, chunk, 0) - far_pair
    cousin_part = swap(grand_part, "node", 2)
    grand_pair = lax.all_gather(
        jnp.concatenate([grand_part, cousin_part], axis=1), "tile", axis=0, tiled=True
    )
    grand_sample, cousin_grand = grand_pair[:, :rank_size], grand_pair[:, rank_size:]
    grand_factor, grand_inverse = factor_pair(
        transposed(grand_sample, grand_sample) + transposed(cousin_grand, cousin_grand)
    )
    grand_transfer = product(grand_sample, grand_inverse.T)
    leaf_out = (basis_rows * math.sqrt(leaf_rows))[None]
    one_rows = lax.dynamic_slice_in_dim(transfer_own, tile * out_rows, out_rows, 0)
    level_one = (one_rows * math.sqrt(2 * rank_size))[None]
    two_rows = product(one_rows, grand_transfer)
    level_two = (two_rows * (2.0 * math.sqrt(rank_size)))[None]
    return (leaf_out, level_one, level_two)


def solution(mesh):
    placed = (P(None, "tile", "node"), P(None, "tile", None))
    return jax.shard_map(
        on_device,
        mesh=mesh,
        in_specs=placed,
        out_specs=(P("node", "tile", None), P("node", "tile", None), P("node", "tile", None)),
        check_vma=False,
    )
```

```python
import functools
import math

import jax
import jax.numpy as jnp
from jax import lax
from jax.experimental import pallas as pl
from jax.experimental.pallas import tpu as pltpu
from jax.sharding import PartitionSpec as P

HIGH = lax.Precision.HIGHEST
MESH = pl.DeviceIdType.MESH
VMEM = pltpu.VMEM


def swap(block, axis, mask):
    count = lax.axis_size(axis)
    return lax.ppermute(block, axis, [(low, low ^ mask) for low in range(count)])


def product(left, right):
    return jnp.dot(left, right, precision=HIGH, preferred_element_type=jnp.float32)


def transposed(left, right):
    return lax.dot_general(
        left, right, (((0,), (0,)), ((), ())), precision=HIGH, preferred_element_type=jnp.float32
    )


def inverse_lower(factor):
    eye = jnp.eye(factor.shape[0], dtype=factor.dtype)
    return jax.scipy.linalg.solve_triangular(factor, eye, lower=True)


def block_kernel(gram_ref, upper_ref, inverse_ref, work_ref):
    size = gram_ref.shape[0]
    work_ref[...] = gram_ref[...]
    lane = lax.broadcasted_iota(jnp.int32, (1, size), 1)
    row = lax.broadcasted_iota(jnp.int32, (size, size), 0)
    inverse_ref[...] = (row == lax.broadcasted_iota(jnp.int32, (size, size), 1)).astype(jnp.float32)

    def step(index, carry):
        current = work_ref[pl.ds(index, 1), :]
        pivot = jnp.sum(jnp.where(lane == index, current, 0.0), axis=1, keepdims=True)
        root = jnp.sqrt(pivot)
        column = jnp.where(lane >= index, current / root, 0.0)
        upper_ref[pl.ds(index, 1), :] = column
        spread = jnp.transpose(jnp.broadcast_to(column, (size, size)))
        work_ref[...] = work_ref[...] - spread * column
        solved = inverse_ref[pl.ds(index, 1), :] / root
        below = jnp.where(row > index, spread, 0.0)
        inverse_ref[...] = inverse_ref[...] - below * solved
        inverse_ref[pl.ds(index, 1), :] = solved
        return carry

    lax.fori_loop(0, size, step, 0)


def factor_block(gram):
    size = gram.shape[0]
    shape = jax.ShapeDtypeStruct((size, size), gram.dtype)
    upper, inverse = pl.pallas_call(
        block_kernel,
        out_shape=(shape, shape),
        in_specs=[pl.BlockSpec(memory_space=VMEM)],
        out_specs=(pl.BlockSpec(memory_space=VMEM), pl.BlockSpec(memory_space=VMEM)),
        scratch_shapes=[VMEM((size, size), gram.dtype)],
    )(gram)
    return upper.T, inverse


def join_lower(upper_left, lower_left, lower_right):
    top = jnp.concatenate([upper_left, jnp.zeros_like(upper_left)], axis=1)
    return jnp.concatenate([top, jnp.concatenate([lower_left, lower_right], axis=1)], axis=0)


def factor_pair(gram, block=128):
    size = gram.shape[0]
    panels = []
    inverses = []
    for start in range(0, size, block):
        stop = start + block
        column = gram[start:, start:stop]
        if panels:
            done = jnp.concatenate(panels, axis=1)
            column = column - product(done[start:], done[start:stop].T)
        diagonal, inverse = factor_block(column[:block])
        inverses.append(inverse)
        below = product(column[block:], inverse.T)
        panel = jnp.concatenate([diagonal, below], axis=0)
        if start:
            panel = jnp.concatenate([jnp.zeros((start, block), gram.dtype), panel], axis=0)
        panels.append(panel)
    factor = jnp.concatenate(panels, axis=1)
    width = block
    while len(inverses) > 1:
        merged = []
        for pair in range(0, len(inverses), 2):
            first, second = inverses[pair], inverses[pair + 1]
            lo = pair * width
            coupling = factor[lo + width:lo + 2 * width, lo:lo + width]
            lower_left = -product(second, product(coupling, first))
            merged.append(join_lower(first, lower_left, second))
        inverses = merged
        width *= 2
    return factor, inverses[0]


def greet(count):
    me = lax.axis_index("tile")
    barrier = pltpu.get_barrier_semaphore()
    for step in range(1, count):
        pl.semaphore_signal(
            barrier, inc=1, device_id={"tile": lax.rem(me + step, count)}, device_id_type=MESH
        )
    pl.semaphore_wait(barrier, count - 1)
    return me


def scatter_kernel(count, block_ref, out_ref, held, send_sem, recv_sem):
    me = greet(count)
    rows = out_ref.shape[0]
    copies = []
    for step in range(1, count):
        target = lax.rem(me + step, count)
        copy = pltpu.make_async_remote_copy(
            src_ref=block_ref.at[pl.ds(pl.multiple_of(target * rows, 8), rows)],
            dst_ref=held.at[step],
            send_sem=send_sem.at[step],
            recv_sem=recv_sem.at[step],
            device_id={"tile": target},
            device_id_type=MESH,
        )
        copy.start()
        copies.append(copy)
    total = block_ref[pl.ds(pl.multiple_of(me * rows, 8), rows), :]
    for step, copy in zip(range(1, count), copies):
        copy.wait()
        total = total + held[step]
    out_ref[...] = total


def gather_kernel(count, block_ref, out_ref, held, send_sem, recv_sem):
    me = greet(count)
    rows = block_ref.shape[0]
    copies = []
    for step in range(1, count):
        target = lax.rem(me + step, count)
        copy = pltpu.make_async_remote_copy(
            src_ref=block_ref,
            dst_ref=held.at[pl.ds(pl.multiple_of(me * rows, 8), rows)],
            send_sem=send_sem.at[step],
            recv_sem=recv_sem.at[step],
            device_id={"tile": target},
            device_id_type=MESH,
        )
        copy.start()
        copies.append(copy)
    out_ref[pl.ds(pl.multiple_of(me * rows, 8), rows), :] = block_ref[...]
    for step, copy in zip(range(1, count), copies):
        copy.wait()
        source = lax.rem(me + count - step, count)
        out_ref[pl.ds(pl.multiple_of(source * rows, 8), rows), :] = held[
            pl.ds(pl.multiple_of(source * rows, 8), rows), :
        ]


def tile_scatter(block, ident):
    count = lax.axis_size("tile")
    rows = block.shape[0] // count
    return pl.pallas_call(
        functools.partial(scatter_kernel, count),
        out_shape=jax.ShapeDtypeStruct((rows, block.shape[1]), block.dtype),
        in_specs=[pl.BlockSpec(memory_space=VMEM)],
        out_specs=pl.BlockSpec(memory_space=VMEM),
        scratch_shapes=[
            VMEM((count, rows, block.shape[1]), block.dtype),
            pltpu.SemaphoreType.DMA((count,)),
            pltpu.SemaphoreType.DMA((count,)),
        ],
        compiler_params=pltpu.CompilerParams(
            collective_id=ident
        ),
    )(block)


def tile_gather(block, ident):
    count = lax.axis_size("tile")
    shape = (block.shape[0] * count, block.shape[1])
    return pl.pallas_call(
        functools.partial(gather_kernel, count),
        out_shape=jax.ShapeDtypeStruct(shape, block.dtype),
        in_specs=[pl.BlockSpec(memory_space=VMEM)],
        out_specs=pl.BlockSpec(memory_space=VMEM),
        scratch_shapes=[
            VMEM(shape, block.dtype),
            pltpu.SemaphoreType.DMA((count,)),
            pltpu.SemaphoreType.DMA((count,)),
        ],
        compiler_params=pltpu.CompilerParams(
            collective_id=ident
        ),
    )(block)


def on_device(schur, samples):
    leaves, slice_cols, leaf_rows = schur.shape
    rank_size = samples.shape[2]
    node = lax.axis_index("node")
    tile = lax.axis_index("tile")
    tile_count = lax.axis_size("tile")
    out_rows = rank_size // tile_count
    owned = lax.dynamic_index_in_dim(samples, node, 0, keepdims=False)
    keep = (jnp.arange(leaves, dtype=jnp.int32) != node)[:, None, None]
    masked = jnp.where(keep, samples, 0.0).reshape(leaves * slice_cols, rank_size)
    stacked = schur.reshape(leaves * slice_cols, leaf_rows)
    sample_rows = lax.psum_scatter(
        transposed(stacked, masked), "tile", scatter_dimension=0, tiled=True
    )
    both = lax.all_gather(
        jnp.concatenate([sample_rows, owned], axis=1), "tile", axis=0, tiled=True
    )
    local = both[:, :rank_size]
    omega = both[:, rank_size:]
    factor, factor_inverse = factor_pair(transposed(local, local))
    basis = product(local, factor_inverse.T)
    reduced = transposed(basis, omega)
    basis_rows = lax.dynamic_slice_in_dim(basis, tile * slice_cols, slice_cols, 0)

    def meet(target):
        piece = lax.dynamic_index_in_dim(schur, target, 0, keepdims=False)
        return product(piece, basis)

    panel_one = product(basis_rows, reduced)
    sibling_rows = swap(panel_one, "node", 1)
    near_meet = meet(jnp.bitwise_xor(node, 1))
    cousin_meet = meet(jnp.bitwise_xor(node, 2))
    further_meet = meet(jnp.bitwise_xor(node, 3))

    near_part = tile_scatter(transposed(near_meet, sibling_rows), 3)
    late_reduced, near_part = lax.optimization_barrier((reduced, near_part))
    other_reduced = swap(late_reduced, "node", 1)
    chunk = near_part.shape[0]
    sample_part = lax.dynamic_slice_in_dim(factor.T, tile * chunk, chunk, 0) - near_part
    other_part = swap(sample_part, "node", 1)
    pair = lax.all_gather(
        jnp.concatenate([sample_part, other_part], axis=1), "tile", axis=0, tiled=True
    )
    parent_sample, other_sample = pair[:, :rank_size], pair[:, rank_size:]
    parent_factor, parent_inverse = factor_pair(
        transposed(parent_sample, parent_sample) + transposed(other_sample, other_sample)
    )
    parent_inverse = parent_inverse.T
    transfer_own = product(parent_sample, parent_inverse)
    transfer_other = product(other_sample, parent_inverse)
    parent_reduced = transposed(transfer_own, reduced) + transposed(transfer_other, other_reduced)
    panel_two = product(basis_rows, product(transfer_own, parent_reduced))
    cousin_rows = swap(panel_two, "node", 2)
    further_rows = swap(panel_two, "node", 3)
    far_sum = transposed(cousin_meet, cousin_rows) + transposed(further_meet, further_rows)
    far_part = tile_scatter(transposed(transfer_own, far_sum), 5)
    far_pair = far_part + swap(far_part, "node", 1)
    grand_part = lax.dynamic_slice_in_dim(parent_factor.T, tile * chunk, chunk, 0) - far_pair
    cousin_part = swap(grand_part, "node", 2)
    grand_pair = lax.all_gather(
        jnp.concatenate([grand_part, cousin_part], axis=1), "tile", axis=0, tiled=True
    )
    grand_sample, cousin_grand = grand_pair[:, :rank_size], grand_pair[:, rank_size:]
    grand_factor, grand_inverse = factor_pair(
        transposed(grand_sample, grand_sample) + transposed(cousin_grand, cousin_grand)
    )
    grand_transfer = product(grand_sample, grand_inverse.T)
    leaf_out = (basis_rows * math.sqrt(leaf_rows))[None]
    one_rows = lax.dynamic_slice_in_dim(transfer_own, tile * out_rows, out_rows, 0)
    level_one = (one_rows * math.sqrt(2 * rank_size))[None]
    two_rows = product(one_rows, grand_transfer)
    level_two = (two_rows * (2.0 * math.sqrt(rank_size)))[None]
    return (leaf_out, level_one, level_two)


def solution(mesh):
    placed = (P(None, "tile", "node"), P(None, "tile", None))
    return jax.shard_map(
        on_device,
        mesh=mesh,
        in_specs=placed,
        out_specs=(P("node", "tile", None), P("node", "tile", None), P("node", "tile", None)),
        check_vma=False,
    )
```

```python
import functools
import math

import jax
import jax.numpy as jnp
from jax import lax
from jax.experimental import pallas as pl
from jax.experimental.pallas import tpu as pltpu
from jax.sharding import PartitionSpec as P

HIGH = lax.Precision.HIGHEST


def swap(block, axis, mask):
    count = lax.axis_size(axis)
    return lax.ppermute(block, axis, [(low, low ^ mask) for low in range(count)])


def product(left, right):
    return jnp.dot(left, right, precision=HIGH, preferred_element_type=jnp.float32)


def transposed(left, right):
    return lax.dot_general(
        left, right, (((0,), (0,)), ((), ())), precision=HIGH, preferred_element_type=jnp.float32
    )


def inverse_lower(factor):
    eye = jnp.eye(factor.shape[0], dtype=factor.dtype)
    return jax.scipy.linalg.solve_triangular(factor, eye, lower=True)


def join_lower(upper_left, lower_left, lower_right):
    top = jnp.concatenate([upper_left, jnp.zeros_like(upper_left)], axis=1)
    return jnp.concatenate([top, jnp.concatenate([lower_left, lower_right], axis=1)], axis=0)


def factor_pair(gram, block=128):
    size = gram.shape[0]
    panels = []
    inverses = []
    for start in range(0, size, block):
        stop = start + block
        column = gram[start:, start:stop]
        if panels:
            done = jnp.concatenate(panels, axis=1)
            column = column - product(done[start:], done[start:stop].T)
        diagonal = jnp.linalg.cholesky(column[:block])
        inverse = inverse_lower(diagonal)
        inverses.append(inverse)
        below = product(column[block:], inverse.T)
        panel = jnp.concatenate([diagonal, below], axis=0)
        if start:
            panel = jnp.concatenate([jnp.zeros((start, block), gram.dtype), panel], axis=0)
        panels.append(panel)
    factor = jnp.concatenate(panels, axis=1)
    width = block
    while len(inverses) > 1:
        merged = []
        for pair in range(0, len(inverses), 2):
            first, second = inverses[pair], inverses[pair + 1]
            lo = pair * width
            coupling = factor[lo + width:lo + 2 * width, lo:lo + width]
            lower_left = -product(second, product(coupling, first))
            merged.append(join_lower(first, lower_left, second))
        inverses = merged
        width *= 2
    return factor, inverses[0]


MESH = pl.DeviceIdType.MESH
VMEM = pltpu.VMEM


def greet(count):
    me = lax.axis_index("tile")
    barrier = pltpu.get_barrier_semaphore()
    for step in range(1, count):
        pl.semaphore_signal(
            barrier, inc=1, device_id={"tile": lax.rem(me + step, count)}, device_id_type=MESH
        )
    pl.semaphore_wait(barrier, count - 1)
    return me


def scatter_kernel(count, block_ref, out_ref, held, send_sem, recv_sem):
    me = greet(count)
    rows = out_ref.shape[0]
    copies = []
    for step in range(1, count):
        target = lax.rem(me + step, count)
        copy = pltpu.make_async_remote_copy(
            src_ref=block_ref.at[pl.ds(pl.multiple_of(target * rows, 8), rows)],
            dst_ref=held.at[step],
            send_sem=send_sem.at[step],
            recv_sem=recv_sem.at[step],
            device_id={"tile": target},
            device_id_type=MESH,
        )
        copy.start()
        copies.append(copy)
    total = block_ref[pl.ds(pl.multiple_of(me * rows, 8), rows), :]
    for step, copy in zip(range(1, count), copies):
        copy.wait()
        total = total + held[step]
    out_ref[...] = total


def gather_kernel(count, block_ref, out_ref, held, send_sem, recv_sem):
    me = greet(count)
    rows = block_ref.shape[0]
    copies = []
    for step in range(1, count):
        target = lax.rem(me + step, count)
        copy = pltpu.make_async_remote_copy(
            src_ref=block_ref,
            dst_ref=held.at[pl.ds(pl.multiple_of(me * rows, 8), rows)],
            send_sem=send_sem.at[step],
            recv_sem=recv_sem.at[step],
            device_id={"tile": target},
            device_id_type=MESH,
        )
        copy.start()
        copies.append(copy)
    out_ref[pl.ds(pl.multiple_of(me * rows, 8), rows), :] = block_ref[...]
    for step, copy in zip(range(1, count), copies):
        copy.wait()
        source = lax.rem(me + count - step, count)
        out_ref[pl.ds(pl.multiple_of(source * rows, 8), rows), :] = held[
            pl.ds(pl.multiple_of(source * rows, 8), rows), :
        ]


def tile_scatter(block, ident):
    count = lax.axis_size("tile")
    rows = block.shape[0] // count
    return pl.pallas_call(
        functools.partial(scatter_kernel, count),
        out_shape=jax.ShapeDtypeStruct((rows, block.shape[1]), block.dtype),
        in_specs=[pl.BlockSpec(memory_space=VMEM)],
        out_specs=pl.BlockSpec(memory_space=VMEM),
        scratch_shapes=[
            VMEM((count, rows, block.shape[1]), block.dtype),
            pltpu.SemaphoreType.DMA((count,)),
            pltpu.SemaphoreType.DMA((count,)),
        ],
        compiler_params=pltpu.CompilerParams(
            collective_id=ident
        ),
    )(block)


def tile_gather(block, ident):
    count = lax.axis_size("tile")
    shape = (block.shape[0] * count, block.shape[1])
    return pl.pallas_call(
        functools.partial(gather_kernel, count),
        out_shape=jax.ShapeDtypeStruct(shape, block.dtype),
        in_specs=[pl.BlockSpec(memory_space=VMEM)],
        out_specs=pl.BlockSpec(memory_space=VMEM),
        scratch_shapes=[
            VMEM(shape, block.dtype),
            pltpu.SemaphoreType.DMA((count,)),
            pltpu.SemaphoreType.DMA((count,)),
        ],
        compiler_params=pltpu.CompilerParams(
            collective_id=ident
        ),
    )(block)


def on_device(schur, samples):
    leaves, slice_cols, leaf_rows = schur.shape
    rank_size = samples.shape[2]
    node = lax.axis_index("node")
    tile = lax.axis_index("tile")
    tile_count = lax.axis_size("tile")
    out_rows = rank_size // tile_count
    owned = lax.dynamic_index_in_dim(samples, node, 0, keepdims=False)
    keep = (jnp.arange(leaves, dtype=jnp.int32) != node)[:, None, None]
    masked = jnp.where(keep, samples, 0.0).reshape(leaves * slice_cols, rank_size)
    stacked = schur.reshape(leaves * slice_cols, leaf_rows)
    sample_rows = lax.psum_scatter(
        transposed(stacked, masked), "tile", scatter_dimension=0, tiled=True
    )
    both = lax.all_gather(
        jnp.concatenate([sample_rows, owned], axis=1), "tile", axis=0, tiled=True
    )
    local = both[:, :rank_size]
    omega = both[:, rank_size:]
    factor, factor_inverse = factor_pair(transposed(local, local))
    reduced = product(factor_inverse, transposed(local, omega))
    local_rows = lax.dynamic_slice_in_dim(local, tile * slice_cols, slice_cols, 0)
    basis_rows = product(local_rows, factor_inverse.T)

    def meet(target):
        piece = lax.dynamic_index_in_dim(schur, target, 0, keepdims=False)
        return product(product(piece, local), factor_inverse.T)

    panel_one = product(basis_rows, reduced)
    sibling_rows = swap(panel_one, "node", 1)
    near_meet = meet(jnp.bitwise_xor(node, 1))
    cousin_meet = meet(jnp.bitwise_xor(node, 2))
    further_meet = meet(jnp.bitwise_xor(node, 3))

    near_part = tile_scatter(transposed(near_meet, sibling_rows), 3)
    late_reduced, near_part = lax.optimization_barrier((reduced, near_part))
    other_reduced = swap(late_reduced, "node", 1)
    chunk = near_part.shape[0]
    sample_part = lax.dynamic_slice_in_dim(factor.T, tile * chunk, chunk, 0) - near_part
    other_part = swap(sample_part, "node", 1)
    pair = lax.all_gather(
        jnp.concatenate([sample_part, other_part], axis=1), "tile", axis=0, tiled=True
    )
    parent_sample, other_sample = pair[:, :rank_size], pair[:, rank_size:]
    parent_factor, parent_inverse = factor_pair(
        transposed(parent_sample, parent_sample) + transposed(other_sample, other_sample)
    )
    parent_inverse = parent_inverse.T
    transfer_own = product(parent_sample, parent_inverse)
    transfer_other = product(other_sample, parent_inverse)
    parent_reduced = transposed(transfer_own, reduced) + transposed(transfer_other, other_reduced)
    panel_two = product(basis_rows, product(transfer_own, parent_reduced))
    cousin_rows = swap(panel_two, "node", 2)
    further_rows = swap(panel_two, "node", 3)
    far_sum = transposed(cousin_meet, cousin_rows) + transposed(further_meet, further_rows)
    far_part = tile_scatter(transposed(transfer_own, far_sum), 5)
    far_pair = far_part + swap(far_part, "node", 1)
    grand_part = lax.dynamic_slice_in_dim(parent_factor.T, tile * chunk, chunk, 0) - far_pair
    cousin_part = swap(grand_part, "node", 2)
    grand_pair = lax.all_gather(
        jnp.concatenate([grand_part, cousin_part], axis=1), "tile", axis=0, tiled=True
    )
    grand_sample, cousin_grand = grand_pair[:, :rank_size], grand_pair[:, rank_size:]
    grand_factor, grand_inverse = factor_pair(
        transposed(grand_sample, grand_sample) + transposed(cousin_grand, cousin_grand)
    )
    grand_transfer = product(grand_sample, grand_inverse.T)
    leaf_out = (basis_rows * math.sqrt(leaf_rows))[None]
    one_rows = lax.dynamic_slice_in_dim(transfer_own, tile * out_rows, out_rows, 0)
    level_one = (one_rows * math.sqrt(2 * rank_size))[None]
    two_rows = product(one_rows, grand_transfer)
    level_two = (two_rows * (2.0 * math.sqrt(rank_size)))[None]
    return (leaf_out, level_one, level_two)


def solution(mesh):
    placed = (P(None, "tile", "node"), P(None, "tile", None))
    return jax.shard_map(
        on_device,
        mesh=mesh,
        in_specs=placed,
        out_specs=(P("node", "tile", None), P("node", "tile", None), P("node", "tile", None)),
        check_vma=False,
    )
```

```python
import functools
import math

import jax
import jax.numpy as jnp
from jax import lax
from jax.experimental import pallas as pl
from jax.experimental.pallas import tpu as pltpu
from jax.sharding import PartitionSpec as P

HIGH = lax.Precision.HIGHEST


def swap(block, axis, mask):
    count = lax.axis_size(axis)
    return lax.ppermute(block, axis, [(low, low ^ mask) for low in range(count)])


def product(left, right):
    return jnp.dot(left, right, precision=HIGH, preferred_element_type=jnp.float32)


def transposed(left, right):
    return lax.dot_general(
        left, right, (((0,), (0,)), ((), ())), precision=HIGH, preferred_element_type=jnp.float32
    )


def inverse_lower(factor):
    eye = jnp.eye(factor.shape[0], dtype=factor.dtype)
    return jax.scipy.linalg.solve_triangular(factor, eye, lower=True)


def join_lower(upper_left, lower_left, lower_right):
    top = jnp.concatenate([upper_left, jnp.zeros_like(upper_left)], axis=1)
    return jnp.concatenate([top, jnp.concatenate([lower_left, lower_right], axis=1)], axis=0)


def factor_pair(gram, block=128):
    size = gram.shape[0]
    panels = []
    inverses = []
    for start in range(0, size, block):
        stop = start + block
        column = gram[start:, start:stop]
        if panels:
            done = jnp.concatenate(panels, axis=1)
            column = column - product(done[start:], done[start:stop].T)
        diagonal = jnp.linalg.cholesky(column[:block])
        inverse = inverse_lower(diagonal)
        inverses.append(inverse)
        below = product(column[block:], inverse.T)
        panel = jnp.concatenate([diagonal, below], axis=0)
        if start:
            panel = jnp.concatenate([jnp.zeros((start, block), gram.dtype), panel], axis=0)
        panels.append(panel)
    factor = jnp.concatenate(panels, axis=1)
    width = block
    while len(inverses) > 1:
        merged = []
        for pair in range(0, len(inverses), 2):
            first, second = inverses[pair], inverses[pair + 1]
            lo = pair * width
            coupling = factor[lo + width:lo + 2 * width, lo:lo + width]
            lower_left = -product(second, product(coupling, first))
            merged.append(join_lower(first, lower_left, second))
        inverses = merged
        width *= 2
    return factor, inverses[0]


MESH = pl.DeviceIdType.MESH
VMEM = pltpu.VMEM


def greet(count):
    me = lax.axis_index("tile")
    barrier = pltpu.get_barrier_semaphore()
    for step in range(1, count):
        pl.semaphore_signal(
            barrier, inc=1, device_id={"tile": lax.rem(me + step, count)}, device_id_type=MESH
        )
    pl.semaphore_wait(barrier, count - 1)
    return me


def scatter_kernel(count, block_ref, out_ref, held, send_sem, recv_sem):
    me = greet(count)
    rows = out_ref.shape[0]
    copies = []
    for step in range(1, count):
        target = lax.rem(me + step, count)
        copy = pltpu.make_async_remote_copy(
            src_ref=block_ref.at[pl.ds(pl.multiple_of(target * rows, 8), rows)],
            dst_ref=held.at[step],
            send_sem=send_sem.at[step],
            recv_sem=recv_sem.at[step],
            device_id={"tile": target},
            device_id_type=MESH,
        )
        copy.start()
        copies.append(copy)
    total = block_ref[pl.ds(pl.multiple_of(me * rows, 8), rows), :]
    for step, copy in zip(range(1, count), copies):
        copy.wait()
        total = total + held[step]
    out_ref[...] = total


def gather_kernel(count, block_ref, out_ref, held, send_sem, recv_sem):
    me = greet(count)
    rows = block_ref.shape[0]
    copies = []
    for step in range(1, count):
        target = lax.rem(me + step, count)
        copy = pltpu.make_async_remote_copy(
            src_ref=block_ref,
            dst_ref=held.at[pl.ds(pl.multiple_of(me * rows, 8), rows)],
            send_sem=send_sem.at[step],
            recv_sem=recv_sem.at[step],
            device_id={"tile": target},
            device_id_type=MESH,
        )
        copy.start()
        copies.append(copy)
    out_ref[pl.ds(pl.multiple_of(me * rows, 8), rows), :] = block_ref[...]
    for step, copy in zip(range(1, count), copies):
        copy.wait()
        source = lax.rem(me + count - step, count)
        out_ref[pl.ds(pl.multiple_of(source * rows, 8), rows), :] = held[
            pl.ds(pl.multiple_of(source * rows, 8), rows), :
        ]


def tile_scatter(block, ident):
    count = lax.axis_size("tile")
    rows = block.shape[0] // count
    return pl.pallas_call(
        functools.partial(scatter_kernel, count),
        out_shape=jax.ShapeDtypeStruct((rows, block.shape[1]), block.dtype),
        in_specs=[pl.BlockSpec(memory_space=VMEM)],
        out_specs=pl.BlockSpec(memory_space=VMEM),
        scratch_shapes=[
            VMEM((count, rows, block.shape[1]), block.dtype),
            pltpu.SemaphoreType.DMA((count,)),
            pltpu.SemaphoreType.DMA((count,)),
        ],
        compiler_params=pltpu.CompilerParams(
            collective_id=ident
        ),
    )(block)


def tile_gather(block, ident):
    count = lax.axis_size("tile")
    shape = (block.shape[0] * count, block.shape[1])
    return pl.pallas_call(
        functools.partial(gather_kernel, count),
        out_shape=jax.ShapeDtypeStruct(shape, block.dtype),
        in_specs=[pl.BlockSpec(memory_space=VMEM)],
        out_specs=pl.BlockSpec(memory_space=VMEM),
        scratch_shapes=[
            VMEM(shape, block.dtype),
            pltpu.SemaphoreType.DMA((count,)),
            pltpu.SemaphoreType.DMA((count,)),
        ],
        compiler_params=pltpu.CompilerParams(
            collective_id=ident
        ),
    )(block)


def on_device(schur, samples):
    leaves, slice_cols, leaf_rows = schur.shape
    rank_size = samples.shape[2]
    node = lax.axis_index("node")
    tile = lax.axis_index("tile")
    tile_count = lax.axis_size("tile")
    out_rows = rank_size // tile_count
    owned = lax.dynamic_index_in_dim(samples, node, 0, keepdims=False)
    keep = (jnp.arange(leaves, dtype=jnp.int32) != node)[:, None, None]
    masked = jnp.where(keep, samples, 0.0).reshape(leaves * slice_cols, rank_size)
    stacked = schur.reshape(leaves * slice_cols, leaf_rows)
    sample_rows = lax.psum_scatter(
        transposed(stacked, masked), "tile", scatter_dimension=0, tiled=True
    )
    both = lax.all_gather(
        jnp.concatenate([sample_rows, owned], axis=1), "tile", axis=0, tiled=True
    )
    local = both[:, :rank_size]
    omega = both[:, rank_size:]
    factor, factor_inverse = factor_pair(transposed(local, local))
    reduced = product(factor_inverse, transposed(local, omega))
    local_rows = lax.dynamic_slice_in_dim(local, tile * slice_cols, slice_cols, 0)
    basis_rows = product(local_rows, factor_inverse.T)

    def meet(target):
        piece = lax.dynamic_index_in_dim(schur, target, 0, keepdims=False)
        return product(product(piece, local), factor_inverse.T)

    panel_one = product(basis_rows, reduced)
    sibling_rows = swap(panel_one, "node", 1)
    near_meet = meet(jnp.bitwise_xor(node, 1))
    cousin_meet = meet(jnp.bitwise_xor(node, 2))
    further_meet = meet(jnp.bitwise_xor(node, 3))

    near_part = tile_scatter(transposed(near_meet, sibling_rows), 3)
    late_reduced, near_part = lax.optimization_barrier((reduced, near_part))
    other_reduced = swap(late_reduced, "node", 1)
    chunk = near_part.shape[0]
    sample_part = lax.dynamic_slice_in_dim(factor.T, tile * chunk, chunk, 0) - near_part
    other_part = swap(sample_part, "node", 1)
    pair = lax.all_gather(
        jnp.concatenate([sample_part, other_part], axis=1), "tile", axis=0, tiled=True
    )
    parent_sample, other_sample = pair[:, :rank_size], pair[:, rank_size:]
    parent_factor, parent_inverse = factor_pair(
        transposed(parent_sample, parent_sample) + transposed(other_sample, other_sample)
    )
    parent_inverse = parent_inverse.T
    transfer_own = product(parent_sample, parent_inverse)
    parent_reduced = product(
        parent_inverse.T,
        transposed(parent_sample, reduced) + transposed(other_sample, other_reduced),
    )
    panel_two = product(basis_rows, product(transfer_own, parent_reduced))
    cousin_rows = swap(panel_two, "node", 2)
    further_rows = swap(panel_two, "node", 3)
    far_sum = transposed(cousin_meet, cousin_rows) + transposed(further_meet, further_rows)
    far_part = tile_scatter(transposed(transfer_own, far_sum), 5)
    far_pair = far_part + swap(far_part, "node", 1)
    grand_part = lax.dynamic_slice_in_dim(parent_factor.T, tile * chunk, chunk, 0) - far_pair
    cousin_part = swap(grand_part, "node", 2)
    grand_pair = lax.all_gather(
        jnp.concatenate([grand_part, cousin_part], axis=1), "tile", axis=0, tiled=True
    )
    grand_sample, cousin_grand = grand_pair[:, :rank_size], grand_pair[:, rank_size:]
    grand_factor, grand_inverse = factor_pair(
        transposed(grand_sample, grand_sample) + transposed(cousin_grand, cousin_grand)
    )
    leaf_out = (basis_rows * math.sqrt(leaf_rows))[None]
    one_rows = lax.dynamic_slice_in_dim(transfer_own, tile * out_rows, out_rows, 0)
    level_one = (one_rows * math.sqrt(2 * rank_size))[None]
    two_rows = product(product(one_rows, grand_sample), grand_inverse.T)
    level_two = (two_rows * (2.0 * math.sqrt(rank_size)))[None]
    return (leaf_out, level_one, level_two)


def solution(mesh):
    placed = (P(None, "tile", "node"), P(None, "tile", None))
    return jax.shard_map(
        on_device,
        mesh=mesh,
        in_specs=placed,
        out_specs=(P("node", "tile", None), P("node", "tile", None), P("node", "tile", None)),
        check_vma=False,
    )
```

```python
import functools
import math

import jax
import jax.numpy as jnp
from jax import lax
from jax.experimental import pallas as pl
from jax.experimental.pallas import tpu as pltpu
from jax.sharding import PartitionSpec as P

HIGH = lax.Precision.HIGHEST


def swap(block, axis, mask):
    count = lax.axis_size(axis)
    return lax.ppermute(block, axis, [(low, low ^ mask) for low in range(count)])


def product(left, right):
    return jnp.dot(left, right, precision=HIGH, preferred_element_type=jnp.float32)


def transposed(left, right):
    return lax.dot_general(
        left, right, (((0,), (0,)), ((), ())), precision=HIGH, preferred_element_type=jnp.float32
    )


def inverse_lower(factor):
    eye = jnp.eye(factor.shape[0], dtype=factor.dtype)
    return jax.scipy.linalg.solve_triangular(factor, eye, lower=True)


def join_lower(upper_left, lower_left, lower_right):
    top = jnp.concatenate([upper_left, jnp.zeros_like(upper_left)], axis=1)
    return jnp.concatenate([top, jnp.concatenate([lower_left, lower_right], axis=1)], axis=0)


def factor_pair(gram, block=128):
    size = gram.shape[0]
    panels = []
    inverses = []
    for start in range(0, size, block):
        stop = start + block
        column = gram[start:, start:stop]
        if panels:
            done = jnp.concatenate(panels, axis=1)
            column = column - product(done[start:], done[start:stop].T)
        diagonal = jnp.linalg.cholesky(column[:block])
        inverse = inverse_lower(diagonal)
        inverses.append(inverse)
        below = product(column[block:], inverse.T)
        panel = jnp.concatenate([diagonal, below], axis=0)
        if start:
            panel = jnp.concatenate([jnp.zeros((start, block), gram.dtype), panel], axis=0)
        panels.append(panel)
    factor = jnp.concatenate(panels, axis=1)
    width = block
    while len(inverses) > 1:
        merged = []
        for pair in range(0, len(inverses), 2):
            first, second = inverses[pair], inverses[pair + 1]
            lo = pair * width
            coupling = factor[lo + width:lo + 2 * width, lo:lo + width]
            lower_left = -product(second, product(coupling, first))
            merged.append(join_lower(first, lower_left, second))
        inverses = merged
        width *= 2
    return factor, inverses[0]


MESH = pl.DeviceIdType.MESH
VMEM = pltpu.VMEM


def greet(count):
    me = lax.axis_index("tile")
    barrier = pltpu.get_barrier_semaphore()
    for step in range(1, count):
        pl.semaphore_signal(
            barrier, inc=1, device_id={"tile": lax.rem(me + step, count)}, device_id_type=MESH
        )
    pl.semaphore_wait(barrier, count - 1)
    return me


def scatter_kernel(count, block_ref, out_ref, held, send_sem, recv_sem):
    me = greet(count)
    rows = out_ref.shape[0]
    copies = []
    for step in range(1, count):
        target = lax.rem(me + step, count)
        copy = pltpu.make_async_remote_copy(
            src_ref=block_ref.at[pl.ds(pl.multiple_of(target * rows, 8), rows)],
            dst_ref=held.at[step],
            send_sem=send_sem.at[step],
            recv_sem=recv_sem.at[step],
            device_id={"tile": target},
            device_id_type=MESH,
        )
        copy.start()
        copies.append(copy)
    total = block_ref[pl.ds(pl.multiple_of(me * rows, 8), rows), :]
    for step, copy in zip(range(1, count), copies):
        copy.wait()
        total = total + held[step]
    out_ref[...] = total


def gather_kernel(count, block_ref, out_ref, held, send_sem, recv_sem):
    me = greet(count)
    rows = block_ref.shape[0]
    copies = []
    for step in range(1, count):
        target = lax.rem(me + step, count)
        copy = pltpu.make_async_remote_copy(
            src_ref=block_ref,
            dst_ref=held.at[pl.ds(pl.multiple_of(me * rows, 8), rows)],
            send_sem=send_sem.at[step],
            recv_sem=recv_sem.at[step],
            device_id={"tile": target},
            device_id_type=MESH,
        )
        copy.start()
        copies.append(copy)
    out_ref[pl.ds(pl.multiple_of(me * rows, 8), rows), :] = block_ref[...]
    for step, copy in zip(range(1, count), copies):
        copy.wait()
        source = lax.rem(me + count - step, count)
        out_ref[pl.ds(pl.multiple_of(source * rows, 8), rows), :] = held[
            pl.ds(pl.multiple_of(source * rows, 8), rows), :
        ]


def tile_scatter(block, ident):
    count = lax.axis_size("tile")
    rows = block.shape[0] // count
    return pl.pallas_call(
        functools.partial(scatter_kernel, count),
        out_shape=jax.ShapeDtypeStruct((rows, block.shape[1]), block.dtype),
        in_specs=[pl.BlockSpec(memory_space=VMEM)],
        out_specs=pl.BlockSpec(memory_space=VMEM),
        scratch_shapes=[
            VMEM((count, rows, block.shape[1]), block.dtype),
            pltpu.SemaphoreType.DMA((count,)),
            pltpu.SemaphoreType.DMA((count,)),
        ],
        compiler_params=pltpu.CompilerParams(
            collective_id=ident
        ),
    )(block)


def tile_gather(block, ident):
    count = lax.axis_size("tile")
    shape = (block.shape[0] * count, block.shape[1])
    return pl.pallas_call(
        functools.partial(gather_kernel, count),
        out_shape=jax.ShapeDtypeStruct(shape, block.dtype),
        in_specs=[pl.BlockSpec(memory_space=VMEM)],
        out_specs=pl.BlockSpec(memory_space=VMEM),
        scratch_shapes=[
            VMEM(shape, block.dtype),
            pltpu.SemaphoreType.DMA((count,)),
            pltpu.SemaphoreType.DMA((count,)),
        ],
        compiler_params=pltpu.CompilerParams(
            collective_id=ident
        ),
    )(block)


def on_device(schur, samples):
    leaves, slice_cols, leaf_rows = schur.shape
    rank_size = samples.shape[2]
    node = lax.axis_index("node")
    tile = lax.axis_index("tile")
    tile_count = lax.axis_size("tile")
    out_rows = rank_size // tile_count
    owned = lax.dynamic_index_in_dim(samples, node, 0, keepdims=False)
    keep = (jnp.arange(leaves, dtype=jnp.int32) != node)[:, None, None]
    masked = jnp.where(keep, samples, 0.0).reshape(leaves * slice_cols, rank_size)
    stacked = schur.reshape(leaves * slice_cols, leaf_rows)
    sample_rows = lax.psum_scatter(
        transposed(stacked, masked), "tile", scatter_dimension=0, tiled=True
    )
    both = lax.all_gather(
        jnp.concatenate([sample_rows, owned], axis=1), "tile", axis=0, tiled=True
    )
    local = both[:, :rank_size]
    omega = both[:, rank_size:]
    factor, factor_inverse = factor_pair(transposed(local, local))
    reduced = product(factor_inverse, transposed(local, omega))
    local_rows = lax.dynamic_slice_in_dim(local, tile * slice_cols, slice_cols, 0)
    basis_rows = product(local_rows, factor_inverse.T)

    def meet(target):
        piece = lax.dynamic_index_in_dim(schur, target, 0, keepdims=False)
        return product(product(piece, local), factor_inverse.T)

    panel_one = product(basis_rows, reduced)
    sibling_rows = swap(panel_one, "node", 1)
    near_meet = meet(jnp.bitwise_xor(node, 1))
    cousin_meet = meet(jnp.bitwise_xor(node, 2))
    further_meet = meet(jnp.bitwise_xor(node, 3))

    near_part = tile_scatter(transposed(near_meet, sibling_rows), 3)
    late_reduced, near_part = lax.optimization_barrier((reduced, near_part))
    other_reduced = swap(late_reduced, "node", 1)
    chunk = near_part.shape[0]
    sample_part = lax.dynamic_slice_in_dim(factor.T, tile * chunk, chunk, 0) - near_part
    other_part = swap(sample_part, "node", 1)
    pair = lax.all_gather(
        jnp.concatenate([sample_part, other_part], axis=1), "tile", axis=0, tiled=True
    )
    parent_sample, other_sample = pair[:, :rank_size], pair[:, rank_size:]
    parent_factor, parent_inverse = factor_pair(
        transposed(parent_sample, parent_sample) + transposed(other_sample, other_sample)
    )
    parent_inverse = parent_inverse.T
    transfer_own = product(parent_sample, parent_inverse)
    transfer_other = product(other_sample, parent_inverse)
    parent_reduced = transposed(transfer_own, reduced) + transposed(transfer_other, other_reduced)
    panel_two = product(basis_rows, product(transfer_own, parent_reduced))
    cousin_rows = swap(panel_two, "node", 2)
    further_rows = swap(panel_two, "node", 3)
    cousin_side = product(cousin_meet, transfer_own)
    further_side = product(further_meet, transfer_own)
    far_sum = transposed(cousin_side, cousin_rows) + transposed(further_side, further_rows)
    far_part = tile_scatter(far_sum, 5)
    far_pair = far_part + swap(far_part, "node", 1)
    grand_part = lax.dynamic_slice_in_dim(parent_factor.T, tile * chunk, chunk, 0) - far_pair
    cousin_part = swap(grand_part, "node", 2)
    grand_pair = lax.all_gather(
        jnp.concatenate([grand_part, cousin_part], axis=1), "tile", axis=0, tiled=True
    )
    grand_sample, cousin_grand = grand_pair[:, :rank_size], grand_pair[:, rank_size:]
    grand_factor, grand_inverse = factor_pair(
        transposed(grand_sample, grand_sample) + transposed(cousin_grand, cousin_grand)
    )
    grand_transfer = product(grand_sample, grand_inverse.T)
    leaf_out = (basis_rows * math.sqrt(leaf_rows))[None]
    one_rows = lax.dynamic_slice_in_dim(transfer_own, tile * out_rows, out_rows, 0)
    level_one = (one_rows * math.sqrt(2 * rank_size))[None]
    two_rows = product(one_rows, grand_transfer)
    level_two = (two_rows * (2.0 * math.sqrt(rank_size)))[None]
    return (leaf_out, level_one, level_two)


def solution(mesh):
    placed = (P(None, "tile", "node"), P(None, "tile", None))
    return jax.shard_map(
        on_device,
        mesh=mesh,
        in_specs=placed,
        out_specs=(P("node", "tile", None), P("node", "tile", None), P("node", "tile", None)),
        check_vma=False,
    )
```

```python
import functools
import math

import jax
import jax.numpy as jnp
from jax import lax
from jax.experimental import pallas as pl
from jax.experimental.pallas import tpu as pltpu
from jax.sharding import PartitionSpec as P

HIGH = lax.Precision.HIGHEST


def swap(block, axis, mask):
    count = lax.axis_size(axis)
    return lax.ppermute(block, axis, [(low, low ^ mask) for low in range(count)])


def product(left, right):
    return jnp.dot(left, right, precision=HIGH, preferred_element_type=jnp.float32)


def transposed(left, right):
    return lax.dot_general(
        left, right, (((0,), (0,)), ((), ())), precision=HIGH, preferred_element_type=jnp.float32
    )


def inverse_lower(factor):
    eye = jnp.eye(factor.shape[0], dtype=factor.dtype)
    return jax.scipy.linalg.solve_triangular(factor, eye, lower=True)


def join_lower(upper_left, lower_left, lower_right):
    top = jnp.concatenate([upper_left, jnp.zeros_like(upper_left)], axis=1)
    return jnp.concatenate([top, jnp.concatenate([lower_left, lower_right], axis=1)], axis=0)


def factor_pair(gram, block=128):
    size = gram.shape[0]
    panels = []
    inverses = []
    for start in range(0, size, block):
        stop = start + block
        column = gram[start:, start:stop]
        if panels:
            done = jnp.concatenate(panels, axis=1)
            column = column - product(done[start:], done[start:stop].T)
        diagonal = jnp.linalg.cholesky(column[:block])
        inverse = inverse_lower(diagonal)
        inverses.append(inverse)
        below = product(column[block:], inverse.T)
        panel = jnp.concatenate([diagonal, below], axis=0)
        if start:
            panel = jnp.concatenate([jnp.zeros((start, block), gram.dtype), panel], axis=0)
        panels.append(panel)
    factor = jnp.concatenate(panels, axis=1)
    width = block
    while len(inverses) > 1:
        merged = []
        for pair in range(0, len(inverses), 2):
            first, second = inverses[pair], inverses[pair + 1]
            lo = pair * width
            coupling = factor[lo + width:lo + 2 * width, lo:lo + width]
            lower_left = -product(second, product(coupling, first))
            merged.append(join_lower(first, lower_left, second))
        inverses = merged
        width *= 2
    return factor, inverses[0]


MESH = pl.DeviceIdType.MESH
VMEM = pltpu.VMEM


def greet(count):
    me = lax.axis_index("tile")
    barrier = pltpu.get_barrier_semaphore()
    for step in range(1, count):
        pl.semaphore_signal(
            barrier, inc=1, device_id={"tile": lax.rem(me + step, count)}, device_id_type=MESH
        )
    pl.semaphore_wait(barrier, count - 1)
    return me


def scatter_kernel(count, block_ref, out_ref, held, send_sem, recv_sem):
    me = greet(count)
    rows = out_ref.shape[0]
    copies = []
    for step in range(1, count):
        target = lax.rem(me + step, count)
        copy = pltpu.make_async_remote_copy(
            src_ref=block_ref.at[pl.ds(pl.multiple_of(target * rows, 8), rows)],
            dst_ref=held.at[step],
            send_sem=send_sem.at[step],
            recv_sem=recv_sem.at[step],
            device_id={"tile": target},
            device_id_type=MESH,
        )
        copy.start()
        copies.append(copy)
    total = block_ref[pl.ds(pl.multiple_of(me * rows, 8), rows), :]
    for step, copy in zip(range(1, count), copies):
        copy.wait()
        total = total + held[step]
    out_ref[...] = total


def gather_kernel(count, block_ref, out_ref, held, send_sem, recv_sem):
    me = greet(count)
    rows = block_ref.shape[0]
    copies = []
    for step in range(1, count):
        target = lax.rem(me + step, count)
        copy = pltpu.make_async_remote_copy(
            src_ref=block_ref,
            dst_ref=held.at[pl.ds(pl.multiple_of(me * rows, 8), rows)],
            send_sem=send_sem.at[step],
            recv_sem=recv_sem.at[step],
            device_id={"tile": target},
            device_id_type=MESH,
        )
        copy.start()
        copies.append(copy)
    out_ref[pl.ds(pl.multiple_of(me * rows, 8), rows), :] = block_ref[...]
    for step, copy in zip(range(1, count), copies):
        copy.wait()
        source = lax.rem(me + count - step, count)
        out_ref[pl.ds(pl.multiple_of(source * rows, 8), rows), :] = held[
            pl.ds(pl.multiple_of(source * rows, 8), rows), :
        ]


def tile_scatter(block, ident):
    count = lax.axis_size("tile")
    rows = block.shape[0] // count
    return pl.pallas_call(
        functools.partial(scatter_kernel, count),
        out_shape=jax.ShapeDtypeStruct((rows, block.shape[1]), block.dtype),
        in_specs=[pl.BlockSpec(memory_space=VMEM)],
        out_specs=pl.BlockSpec(memory_space=VMEM),
        scratch_shapes=[
            VMEM((count, rows, block.shape[1]), block.dtype),
            pltpu.SemaphoreType.DMA((count,)),
            pltpu.SemaphoreType.DMA((count,)),
        ],
        compiler_params=pltpu.CompilerParams(
            collective_id=ident
        ),
    )(block)


def tile_gather(block, ident):
    count = lax.axis_size("tile")
    shape = (block.shape[0] * count, block.shape[1])
    return pl.pallas_call(
        functools.partial(gather_kernel, count),
        out_shape=jax.ShapeDtypeStruct(shape, block.dtype),
        in_specs=[pl.BlockSpec(memory_space=VMEM)],
        out_specs=pl.BlockSpec(memory_space=VMEM),
        scratch_shapes=[
            VMEM(shape, block.dtype),
            pltpu.SemaphoreType.DMA((count,)),
            pltpu.SemaphoreType.DMA((count,)),
        ],
        compiler_params=pltpu.CompilerParams(
            collective_id=ident
        ),
    )(block)


def on_device(schur, samples):
    leaves, slice_cols, leaf_rows = schur.shape
    rank_size = samples.shape[2]
    node = lax.axis_index("node")
    tile = lax.axis_index("tile")
    tile_count = lax.axis_size("tile")
    out_rows = rank_size // tile_count
    owned = lax.dynamic_index_in_dim(samples, node, 0, keepdims=False)
    keep = (jnp.arange(leaves, dtype=jnp.int32) != node)[:, None, None]
    masked = jnp.where(keep, samples, 0.0).reshape(leaves * slice_cols, rank_size)
    stacked = schur.reshape(leaves * slice_cols, leaf_rows)
    sample_rows = lax.psum_scatter(
        transposed(stacked, masked), "tile", scatter_dimension=0, tiled=True
    )
    both = lax.all_gather(
        jnp.concatenate([sample_rows, owned], axis=1), "tile", axis=0, tiled=True
    )
    local = both[:, :rank_size]
    omega = both[:, rank_size:]
    factor, factor_inverse = factor_pair(transposed(local, local))
    reduced = product(factor_inverse, transposed(local, omega))
    local_rows = lax.dynamic_slice_in_dim(local, tile * slice_cols, slice_cols, 0)
    basis_rows = product(local_rows, factor_inverse.T)

    def meet(target):
        piece = lax.dynamic_index_in_dim(schur, target, 0, keepdims=False)
        return product(product(piece, local), factor_inverse.T)

    panel_one = product(basis_rows, reduced)
    sibling_rows = swap(panel_one, "node", 1)
    near_meet = meet(jnp.bitwise_xor(node, 1))
    cousin_meet = meet(jnp.bitwise_xor(node, 2))
    further_meet = meet(jnp.bitwise_xor(node, 3))

    near_part = tile_scatter(transposed(near_meet, sibling_rows), 3)
    late_reduced, near_part = lax.optimization_barrier((reduced, near_part))
    other_reduced = swap(late_reduced, "node", 1)
    chunk = near_part.shape[0]
    sample_part = lax.dynamic_slice_in_dim(factor.T, tile * chunk, chunk, 0) - near_part
    other_part = swap(sample_part, "node", 1)
    pair = lax.all_gather(
        jnp.concatenate([sample_part, other_part], axis=1), "tile", axis=0, tiled=True
    )
    parent_sample, other_sample = pair[:, :rank_size], pair[:, rank_size:]
    parent_factor, parent_inverse = factor_pair(
        transposed(parent_sample, parent_sample) + transposed(other_sample, other_sample)
    )
    parent_inverse = parent_inverse.T
    transfer_own = product(parent_sample, parent_inverse)
    transfer_other = product(other_sample, parent_inverse)
    parent_reduced = transposed(transfer_own, reduced) + transposed(transfer_other, other_reduced)
    panel_two = product(basis_rows, product(transfer_own, parent_reduced))
    cousin_rows = swap(panel_two, "node", 2)
    further_rows = swap(panel_two, "node", 3)
    cousin_side = product(cousin_meet, transfer_own)
    further_side = product(further_meet, transfer_own)
    far_sum = transposed(cousin_side, cousin_rows) + transposed(further_side, further_rows)
    far_part = tile_scatter(far_sum, 5)
    far_pair = far_part + swap(far_part, "node", 1)
    grand_part = lax.dynamic_slice_in_dim(parent_factor.T, tile * chunk, chunk, 0) - far_pair
    cousin_part = swap(grand_part, "node", 2)
    grand_pair = lax.all_gather(
        jnp.concatenate([grand_part, cousin_part], axis=1), "tile", axis=0, tiled=True
    )
    grand_sample, cousin_grand = grand_pair[:, :rank_size], grand_pair[:, rank_size:]
    grand_factor, grand_inverse = factor_pair(
        transposed(grand_sample, grand_sample) + transposed(cousin_grand, cousin_grand)
    )
    leaf_out = (basis_rows * math.sqrt(leaf_rows))[None]
    one_rows = lax.dynamic_slice_in_dim(transfer_own, tile * out_rows, out_rows, 0)
    level_one = (one_rows * math.sqrt(2 * rank_size))[None]
    two_rows = product(product(one_rows, grand_sample), grand_inverse.T)
    level_two = (two_rows * (2.0 * math.sqrt(rank_size)))[None]
    return (leaf_out, level_one, level_two)


def solution(mesh):
    placed = (P(None, "tile", "node"), P(None, "tile", None))
    return jax.shard_map(
        on_device,
        mesh=mesh,
        in_specs=placed,
        out_specs=(P("node", "tile", None), P("node", "tile", None), P("node", "tile", None)),
        check_vma=False,
    )
```
